32 devices in a mesh: dp: 4 (over y, core), ctx: 2 (over x), tensor: 4 (over z).
Axes of the slice: x: 2, y: 2, z: 4, core: 2. Of those that a mesh axis runs over, the one named last changes fastest.
Arguments:
- layer_input: bfloat16 [4, 512, 8192], P('dp', ('ctx', 'tensor')), may hold values from -6 to 6
- queries: bfloat16 [4, 512, 8192], P('dp', 'ctx', 'tensor'), may hold values from -12 to 12
- forward_output: bfloat16 [4, 512, 8192], P('dp', 'ctx', 'tensor'), may hold values from -6 to 6
- attention_output_gradient: bfloat16 [4, 512, 8192], P('dp', 'ctx', 'tensor'), may hold values from -6 to 6
- key_weight: bfloat16 [8192, 1024], P(None, 'tensor'), may hold values from -3 to 3
- value_projection_weight: bfloat16 [8192, 1024], P(None, 'tensor'), may hold values from -0.0625 to 0.0625
- segment: int32 [4, 512], P('dp'), may hold values from 0 to 4, as said below
- block_table: int32 [4, 4, 4], P('dp'), may hold values from 0 to 1, as said below
- block_owner: int32 [4, 4], P('dp'), may hold values from 0 to 3, each once within a row
Outputs:
- query_grad: bfloat16 [4, 512, 8192], P('dp', 'ctx', 'tensor')
- input_grad: bfloat16 [4, 512, 8192], P('dp', ('ctx', 'tensor'))
- key_weight_grad: bfloat16 [8192, 1024], P(('dp', 'ctx'), 'tensor')
- value_weight_grad: bfloat16 [8192, 1024], P(('dp', 'ctx'), 'tensor')
The draws below stay inside these ranges and needn't reach their ends.
Inputs may be any that keep to these rules, and one draw needn't show every extreme that they name: Along the logical positions of a group the segment never falls; the prompt (0) comes first and every rollout 1 to 4 is present. block_table[g, b, c] is 1 only where some position of logical block b may read some position of logical block c under the causal and segment rule; block_table[g, b, b] is 1 for every block; other such pairs may be 0. `block_owner`: each group's row holds every logical block once.
All inputs are finite; a program needn't handle non-finite values.
Results may differ from the reference program's by a relative error of at most 0.005.
The reference program's roundings to bfloat16 on the way (of `probs_low` and `score_low`) count: a program that leaves them out, or rounds other values in their place, can miss the bound.
Values may be sent and summed in bfloat16 or wider, within the bound.
A program may use at most 128 MiB of HBM per device.

```python
import math
import jax
import jax.numpy as jnp
from jax import lax

MODEL_WIDTH = 8192
QUERY_HEADS = 64
KEY_VALUE_HEADS = 8
HEAD_SIZE = 128
BLK = 128
NROLL = 4
GROUPS = 4
PACK_TOKENS = 512
NBLK = 4


def truncated_gaussian(key, shape, bound):
    return jnp.clip(jax.random.normal(key, shape, jnp.float32), -bound, bound)


def draw_layer_input(key, part):
    random_seed_key = jax.random.fold_in(key, 11)
    value_tensor = truncated_gaussian(random_seed_key, (GROUPS, PACK_TOKENS, MODEL_WIDTH), 6.0)
    return value_tensor.astype(jnp.bfloat16)


def draw_key_weight(key, part):
    random_seed_key = jax.random.fold_in(key, 21)
    fanin_scale = MODEL_WIDTH ** (-0.5)
    value_tensor = truncated_gaussian(random_seed_key, (MODEL_WIDTH, KEY_VALUE_HEADS * HEAD_SIZE), 6.0) * fanin_scale
    return value_tensor.astype(jnp.bfloat16)


def draw_queries(key, part):
    random_seed_key = jax.random.fold_in(key, 31)
    value_tensor = truncated_gaussian(random_seed_key, (GROUPS, PACK_TOKENS, QUERY_HEADS * HEAD_SIZE), 6.0)
    return value_tensor.astype(jnp.bfloat16)


def tree_layout(key):
    layout_key = jax.random.fold_in(key, 55)
    prompt_jit = max(1, min(BLK // 2, PACK_TOKENS // 32))
    prompt_len = PACK_TOKENS * 5 // 8 + jax.random.randint(jax.random.fold_in(layout_key, 1), (GROUPS, 1), -prompt_jit, prompt_jit + 1)
    remaining = PACK_TOKENS - prompt_len
    roll_jit = max(1, min(BLK // 4, (PACK_TOKENS - PACK_TOKENS * 5 // 8 - prompt_jit) // 16))
    positions = jnp.arange(PACK_TOKENS, dtype=jnp.int32)[None, :]
    segments = jnp.where(positions >= prompt_len, 1, 0).astype(jnp.int32)
    for rollout in range(1, NROLL):
        jitter = jax.random.randint(jax.random.fold_in(layout_key, 10 + rollout), (GROUPS, 1), -roll_jit, roll_jit + 1)
        boundary = prompt_len + remaining * rollout // NROLL + jitter
        segments = segments + jnp.where(positions >= boundary, 1, 0).astype(jnp.int32)
    return segments


def draw_segment(key, part):
    return tree_layout(key)


def draw_block_table(key, part):
    segments = tree_layout(key)
    positions = jnp.arange(PACK_TOKENS, dtype=jnp.int32)
    causal = positions[None, :] <= positions[:, None]
    readable = causal[None] & ((segments[:, None, :] == 0) | (segments[:, None, :] == segments[:, :, None]))
    blocks = readable.reshape(GROUPS, NBLK, BLK, NBLK, BLK).any(axis=(2, 4))
    withheld = jax.random.randint(jax.random.fold_in(key, 77), (GROUPS, NBLK, NBLK), 0, 4) == 0
    diagonal = jnp.arange(NBLK)[:, None] == jnp.arange(NBLK)[None, :]
    blocks = blocks & (jnp.logical_not(withheld) | diagonal[None])
    return jnp.where(blocks, 1, 0).astype(jnp.int32)


def level_of(rng, extent, shards, low, largest):
    level = 1.0
    for position, shards_of in shards:
        heights = jax.random.uniform(jax.random.fold_in(jax.random.fold_in(rng, 6), position), (shards_of,), jnp.float32, low / len(shards), largest / len(shards))
        level = level * jnp.repeat(jnp.exp(heights), extent[position] // shards_of).reshape((-1,) + (1,) * (len(extent) - 1 - position))
    return level


def gaussian(stream_key, extent, scale, most, shards=(), kind=jnp.bfloat16):
    result = jax.random.normal(stream_key, extent, jnp.float32) * scale
    if len(shards) > 0:
        result = level_of(stream_key, extent, shards, -0.22, 0.18) * result
    return jnp.clip(result, min=-most, max=most).astype(kind)


def setup_inputs(seed: int = 0) -> dict:
    seeds = jax.random.split(jax.random.key(seed), 10)
    return {
        "layer_input": draw_layer_input(jax.random.fold_in(seeds[9], 71), 0),
        "queries": draw_queries(jax.random.fold_in(seeds[9], 71), 0),
        "forward_output": gaussian(seeds[2], (GROUPS, PACK_TOKENS, QUERY_HEADS * HEAD_SIZE), 1.0, 6.0, ((0, 4), (1, 2), (2, 4))),
        "attention_output_gradient": gaussian(seeds[3], (GROUPS, PACK_TOKENS, QUERY_HEADS * HEAD_SIZE), 1.0, 6.0, ((0, 4), (1, 2), (2, 4))),
        "key_weight": draw_key_weight(jax.random.fold_in(seeds[9], 71), 0),
        "value_projection_weight": gaussian(seeds[5], (MODEL_WIDTH, KEY_VALUE_HEADS * HEAD_SIZE), MODEL_WIDTH ** -0.5, 0.0625, ((1, 4),)),
        "segment": draw_segment(jax.random.fold_in(seeds[9], 71), 0),
        "block_table": draw_block_table(jax.random.fold_in(seeds[9], 71), 0),
        "block_owner": jax.vmap(lambda own: jax.random.permutation(own, NBLK))(jax.random.split(seeds[8], GROUPS)).reshape((GROUPS, NBLK)).astype(jnp.int32),
    }


def head_grads(scan_entries, allowed):
    query_h, key_h, value_h, saved_h, grad_h = scan_entries
    softmax_scale = 1.0 / math.sqrt(HEAD_SIZE)
    query_f = query_h.astype(jnp.float32)
    key_f = key_h.astype(jnp.float32)
    value_f = value_h.astype(jnp.float32)
    grad_f = grad_h.astype(jnp.float32)
    scores = jnp.einsum('igd,jd->gij', query_f, key_f) * softmax_scale
    scores = jnp.where(allowed[None], scores, -jnp.inf)
    row_max = lax.optimization_barrier(jnp.max(scores, axis=-1, keepdims=True))
    log_norm = row_max + jnp.log(lax.optimization_barrier(jnp.sum(jnp.exp(scores - row_max), axis=-1, keepdims=True)))
    probabilities = jnp.exp(scores - log_norm)
    probs_low = lax.optimization_barrier(probabilities.astype(jnp.bfloat16)).astype(jnp.float32)
    value_gradient_rows = jnp.einsum('gij,igd->jd', probs_low, grad_f)
    prob_grads = jnp.einsum('igd,jd->gij', grad_f, value_f)
    correction = lax.optimization_barrier(jnp.sum(grad_f * saved_h.astype(jnp.float32), axis=-1)).T
    score_low = (probabilities * (prob_grads - correction[:, :, None])).astype(jnp.bfloat16)
    score_low = lax.optimization_barrier(score_low).astype(jnp.float32)
    query_grads = jnp.einsum('gij,jd->igd', score_low, key_f) * softmax_scale
    key_gradient_rows = jnp.einsum('gij,igd->jd', score_low, query_f) * softmax_scale
    return (query_grads, key_gradient_rows, value_gradient_rows)

def reference(layer_input, queries, forward_output, attention_output_gradient, key_weight, value_projection_weight, segment, block_table, block_owner):
    queries_per_group = QUERY_HEADS // KEY_VALUE_HEADS
    query_outs = []
    input_outs = []
    key_weight_total = jnp.zeros((MODEL_WIDTH, KEY_VALUE_HEADS * HEAD_SIZE), jnp.float32)
    value_weight_total = jnp.zeros((MODEL_WIDTH, KEY_VALUE_HEADS * HEAD_SIZE), jnp.float32)
    for head_group in range(GROUPS):
        group_input = layer_input[head_group]
        projected_keys = jnp.dot(group_input, key_weight, preferred_element_type=jnp.float32).astype(jnp.bfloat16)
        projected_values = jnp.dot(group_input, value_projection_weight, preferred_element_type=jnp.float32).astype(jnp.bfloat16)
        row_ids = jnp.arange(PACK_TOKENS, dtype=jnp.int32)
        positions = block_owner[head_group][row_ids // BLK].astype(jnp.int32) * BLK + row_ids % BLK
        segments_at = segment[head_group][positions]
        block_of = positions // BLK
        allowed = positions[None, :] <= positions[:, None]
        allowed = allowed & ((segments_at[None, :] == 0) | (segments_at[None, :] == segments_at[:, None]))
        allowed = allowed & (block_table[head_group][block_of[:, None], block_of[None, :]] == 1)

        def separate_heads(numeric_array):
            return numeric_array.reshape(PACK_TOKENS, KEY_VALUE_HEADS, queries_per_group, HEAD_SIZE).transpose(1, 0, 2, 3)
        scan_entries = (separate_heads(queries[head_group]), projected_keys.reshape(PACK_TOKENS, KEY_VALUE_HEADS, HEAD_SIZE).transpose(1, 0, 2), projected_values.reshape(PACK_TOKENS, KEY_VALUE_HEADS, HEAD_SIZE).transpose(1, 0, 2), separate_heads(forward_output[head_group]), separate_heads(attention_output_gradient[head_group]))
        query_grads, key_gradient_rows, value_gradient_rows = lax.map(lambda entry: head_grads(entry, allowed), scan_entries)
        query_outs.append(query_grads.transpose(1, 0, 2, 3).reshape(PACK_TOKENS, QUERY_HEADS * HEAD_SIZE).astype(jnp.bfloat16))
        key_reduced = key_gradient_rows.transpose(1, 0, 2).reshape(PACK_TOKENS, KEY_VALUE_HEADS * HEAD_SIZE).astype(jnp.bfloat16)
        value_reduced = value_gradient_rows.transpose(1, 0, 2).reshape(PACK_TOKENS, KEY_VALUE_HEADS * HEAD_SIZE).astype(jnp.bfloat16)
        input_sum = jnp.dot(key_reduced, key_weight.T, preferred_element_type=jnp.float32)
        input_sum = input_sum + jnp.dot(value_reduced, value_projection_weight.T, preferred_element_type=jnp.float32)
        input_outs.append(input_sum.astype(jnp.bfloat16))
        key_weight_total = key_weight_total + jnp.dot(group_input.T, key_reduced, preferred_element_type=jnp.float32)
        value_weight_total = value_weight_total + jnp.dot(group_input.T, value_reduced, preferred_element_type=jnp.float32)
    return (jnp.stack(query_outs), jnp.stack(input_outs), key_weight_total.astype(jnp.bfloat16), value_weight_total.astype(jnp.bfloat16))
```

```python
import math

import jax
import jax.numpy as jnp
from jax import lax
from jax.sharding import PartitionSpec as P

HEAD_SIZE = 128
BLK = 128


def per_device(
    layer_input,
    queries,
    forward_output,
    attention_output_gradient,
    key_weight,
    value_projection_weight,
    segment,
    block_table,
    block_owner,
):
    softmax_scale = 1.0 / math.sqrt(HEAD_SIZE)
    local_rows = queries.shape[1]
    kv_local = key_weight.shape[1] // HEAD_SIZE
    q_local = queries.shape[2] // HEAD_SIZE
    queries_per_group = q_local // kv_local
    kv_width = kv_local * HEAD_SIZE
    gathered = lax.all_gather(layer_input, "tensor", axis=1, tiled=True)[0]
    planes = lax.axis_size("tensor")
    plane_size = lax.axis_size("dp") * lax.axis_size("ctx")
    plane_index = lax.axis_index("dp") * lax.axis_size("ctx") + lax.axis_index("ctx")
    model_width = key_weight.shape[0]
    piece_rows = model_width // (planes * plane_size)

    def piece(weight):
        split = weight.reshape(planes, plane_size, piece_rows, kv_width)
        return lax.dynamic_index_in_dim(split, plane_index, 1, keepdims=False)

    pieces = jnp.concatenate([piece(key_weight), piece(value_projection_weight)], axis=2)
    pieces = lax.all_to_all(pieces, "tensor", split_axis=0, concat_axis=0, tiled=True)
    wide_weight = lax.all_gather(pieces, ("dp", "ctx"), axis=1, tiled=True)
    plane_input = lax.all_to_all(gathered, ("dp", "ctx"), split_axis=1, concat_axis=0, tiled=True)
    projected_keys = jnp.dot(gathered, key_weight, preferred_element_type=jnp.float32)
    projected_values = jnp.dot(
        gathered, value_projection_weight, preferred_element_type=jnp.float32
    )
    kv_rows = jnp.concatenate([projected_keys, projected_values], axis=1).astype(jnp.bfloat16)
    owner_row = block_owner[0]
    segments_row = segment[0]
    table_row = block_table[0]
    blocks_here = local_rows // BLK
    ctx_index = lax.axis_index("ctx")
    own_blocks = lax.dynamic_slice_in_dim(owner_row, ctx_index * blocks_here, blocks_here)
    offsets = jnp.arange(BLK, dtype=jnp.int32)
    query_pos = (own_blocks[:, None] * BLK + offsets[None, :]).reshape(-1)
    query_seg = jnp.take(segments_row, query_pos)
    own_table = jnp.take(table_row, own_blocks, axis=0)
    query_heads = queries[0].reshape(local_rows, kv_local, queries_per_group, HEAD_SIZE)
    grad_heads = attention_output_gradient[0].reshape(
        local_rows, kv_local, queries_per_group, HEAD_SIZE
    )
    saved_heads = forward_output[0].reshape(local_rows, kv_local, queries_per_group, HEAD_SIZE)
    correction = jnp.sum(grad_heads.astype(jnp.float32) * saved_heads.astype(jnp.float32), axis=-1)
    correction = correction.transpose(1, 2, 0)

    def allowed_for(leading_row, row_count):
        key_blocks = lax.dynamic_slice_in_dim(owner_row, leading_row // BLK, row_count // BLK)
        key_pos = (key_blocks[:, None] * BLK + offsets[None, :]).reshape(-1)
        key_seg = jnp.take(segments_row, key_pos)
        table_part = jnp.take(own_table, key_blocks, axis=1) == 1
        table_full = jnp.broadcast_to(
            table_part[:, None, :, None], (blocks_here, BLK, row_count // BLK, BLK)
        )
        table_full = table_full.reshape(local_rows, row_count)
        same_tree = (key_seg[None, :] == 0) | (key_seg[None, :] == query_seg[:, None])
        return table_full & (key_pos[None, :] <= query_pos[:, None]) & same_tree

    def block_scores(block_rows, leading_row):
        row_count = block_rows.shape[0]
        block_keys = block_rows[:, :kv_width].reshape(row_count, kv_local, HEAD_SIZE)
        block_values = block_rows[:, kv_width:].reshape(row_count, kv_local, HEAD_SIZE)
        raw_scores = (
            jnp.einsum(
                "qhgd,khd->hgqk", query_heads, block_keys, preferred_element_type=jnp.float32
            )
            * softmax_scale
        )
        allowed = allowed_for(leading_row, row_count)
        return (jnp.where(allowed[None, None], raw_scores, -jnp.inf), block_keys, block_values)

    def stats_block(carried, block_rows, leading_row):
        running_max, running_sum = carried
        scores = block_scores(block_rows, leading_row)[0]
        new_max = jnp.maximum(running_max, jnp.max(scores, axis=-1))
        running_sum = running_sum * jnp.exp(running_max - new_max) + jnp.sum(
            jnp.exp(scores - new_max[..., None]), axis=-1
        )
        return (new_max, running_sum)

    def grads_block(carried, block_rows, leading_row, log_norm):
        query_sum, keyval_sum = carried
        row_count = block_rows.shape[0]
        scores, block_keys, block_values = block_scores(block_rows, leading_row)
        probabilities = jnp.exp(scores - log_norm[..., None])
        probs_low = probabilities.astype(jnp.bfloat16)
        value_gradient_rows = jnp.einsum(
            "hgqk,qhgd->khd", probs_low, grad_heads, preferred_element_type=jnp.float32
        )
        prob_grads = jnp.einsum(
            "qhgd,khd->hgqk", grad_heads, block_values, preferred_element_type=jnp.float32
        )
        score_low = (probabilities * (prob_grads - correction[..., None])).astype(jnp.bfloat16)
        query_sum = query_sum + jnp.einsum(
            "hgqk,khd->qhgd", score_low, block_keys, preferred_element_type=jnp.float32
        )
        key_gradient_rows = (
            jnp.einsum("hgqk,qhgd->khd", score_low, query_heads, preferred_element_type=jnp.float32)
            * softmax_scale
        )
        update = jnp.concatenate(
            [
                key_gradient_rows.reshape(row_count, kv_width),
                value_gradient_rows.reshape(row_count, kv_width),
            ],
            axis=1,
        )
        keyval_sum = lax.dynamic_update_slice_in_dim(keyval_sum, update, leading_row, 0)
        return (query_sum, keyval_sum)

    def over_blocks(block_step, carried, shard_part):
        row_count = shard_part.shape[0]
        block_size = math.gcd(row_count, max(512, local_rows))
        block_count = row_count // block_size
        pieces = shard_part.reshape(block_count, block_size, shard_part.shape[1])
        starts = block_size * jnp.arange(block_count, dtype=jnp.int32)

        def one_block(state_in, scan_item):
            block_rows, block_start = scan_item
            result = block_step(state_in, block_rows, block_start)
            return (result, None)

        carried, _ = lax.scan(one_block, carried, (pieces, starts))
        return carried

    stats_init = (
        jnp.full((kv_local, queries_per_group, local_rows), -1e30, jnp.float32),
        jnp.zeros((kv_local, queries_per_group, local_rows), jnp.float32),
    )
    seq_rows = local_rows * lax.axis_size("ctx")
    grads_init = (
        jnp.zeros((local_rows, kv_local, queries_per_group, HEAD_SIZE), jnp.float32),
        jnp.zeros((seq_rows, 2 * kv_width), jnp.float32),
    )
    running_max, running_sum = over_blocks(
        stats_block, stats_init, lax.all_gather(kv_rows, "ctx", axis=0, tiled=True)
    )
    log_norm = running_max + jnp.log(running_sum)

    def grads_fold(carried, shard_part):
        return over_blocks(
            lambda state, rows_in, start_in: grads_block(state, rows_in, start_in, log_norm),
            carried,
            shard_part,
        )

    query_sum, keyval_sum = grads_fold(
        grads_init, lax.all_gather(kv_rows, "ctx", axis=0, tiled=True)
    )
    own_grads = lax.psum_scatter(keyval_sum, "ctx", scatter_dimension=0, tiled=True).astype(
        jnp.bfloat16
    )
    query_grad = (
        (query_sum * softmax_scale).astype(jnp.bfloat16).reshape(1, local_rows, q_local * HEAD_SIZE)
    )
    kv_all = lax.all_gather(own_grads, "tensor", axis=0)
    kv_plane = lax.all_gather(own_grads, ("dp", "ctx"), axis=0, tiled=True)
    width_part = lax.dot_general(
        kv_all, wide_weight, (((0, 2), (0, 2)), ((), ())), preferred_element_type=jnp.float32
    ).astype(jnp.bfloat16)
    input_grad = lax.all_to_all(width_part, "tensor", split_axis=0, concat_axis=1, tiled=True)[None]
    weight_sum = lax.dot_general(
        plane_input, kv_plane, (((0,), (0,)), ((), ())), preferred_element_type=jnp.float32
    )
    key_weight_grad = weight_sum[:, :kv_width].astype(jnp.bfloat16)
    value_weight_grad = weight_sum[:, kv_width:].astype(jnp.bfloat16)
    return (query_grad, input_grad, key_weight_grad, value_weight_grad)


def solution(mesh):
    in_specs = (
        P("dp", ("ctx", "tensor"), None),
        P("dp", "ctx", "tensor"),
        P("dp", "ctx", "tensor"),
        P("dp", "ctx", "tensor"),
        P(None, "tensor"),
        P(None, "tensor"),
        P("dp", None),
        P("dp", None, None),
        P("dp", None),
    )
    out_specs = (
        P("dp", "ctx", "tensor"),
        P("dp", ("ctx", "tensor"), None),
        P(("dp", "ctx"), "tensor"),
        P(("dp", "ctx"), "tensor"),
    )
    return jax.shard_map(
        per_device, mesh=mesh, in_specs=in_specs, out_specs=out_specs, check_vma=False
    )
```

```python
import functools
import math

import jax
import jax.numpy as jnp
from jax import lax
from jax.experimental import pallas as pl
from jax.experimental.pallas import tpu as pltpu
from jax.sharding import PartitionSpec as P

HEAD_SIZE = 128
BLK = 128

MESH = pl.DeviceIdType.MESH


def exchange_kernel(
    nt, nd, nc, x_ref, kw_ref, vw_ref, g_ref, xc_ref, wide_ref,
    x_send, x_recv, w_send, w_recv, p_send, p_recv, f_send, f_recv, s_send, s_recv, local_sem,
):
    t = lax.axis_index("tensor")
    d = lax.axis_index("dp")
    c = lax.axis_index("ctx")
    plane = nd * nc
    half = plane // 2
    p = d * nc + c
    h = (d // 2) * nc + c
    core = d % 2
    rows, width = x_ref.shape
    kv = kw_ref.shape[1]
    chunk = width // nt
    piece = chunk // plane
    slice_width = width // plane

    barrier = pltpu.get_barrier_semaphore()
    for r in range(1, nt):
        pl.semaphore_signal(
            barrier, inc=1, device_id={"tensor": (t + r) % nt}, device_id_type=MESH
        )
    for r in range(1, plane):
        q = (p + r) % plane
        pl.semaphore_signal(
            barrier, inc=1, device_id={"dp": q // nc, "ctx": q % nc}, device_id_type=MESH
        )
    pl.semaphore_wait(barrier, nt - 1 + plane - 1)

    def x_rows(b):
        return g_ref.at[pl.ds(pl.multiple_of(b * rows, rows), rows), :]

    def x_copy(way, s, source, b, target):
        return pltpu.make_async_remote_copy(
            src_ref=source, dst_ref=x_rows(b), send_sem=x_send.at[way, s - 1],
            recv_sem=x_recv.at[way, s - 1], device_id={"tensor": target}, device_id_type=MESH,
        )

    def sends(s):
        for way in (0, 1):
            step = 1 if way == 0 else -1
            b = t - step * (s - 1)
            target = t + step
            ok = (target >= 0) & (target < nt) & (b >= 0) & (b < nt)
            yield way, ok, b, target

    def start_x(s):
        for way, ok, b, target in sends(s):
            @pl.when(ok)
            def _():
                x_copy(way, s, x_ref if s == 1 else x_rows(b), b, target).start()

    def w_copy(which, r):
        other = (t + r) % nt
        source = (kw_ref, vw_ref)[which].at[
            pl.ds(pl.multiple_of(other * chunk + p * piece, piece), piece), :
        ]
        return pltpu.make_async_remote_copy(
            src_ref=source,
            dst_ref=wide_ref.at[
                t, pl.ds(pl.multiple_of(p * piece, piece), piece), pl.ds(which * kv, kv)
            ],
            send_sem=w_send.at[which, r - 1], recv_sem=w_recv.at[which, r - 1],
            device_id={"tensor": other}, device_id_type=MESH,
        )

    def plane_copy(b, r, source):
        q = (p + r) % plane
        return pltpu.make_async_remote_copy(
            src_ref=source.at[:, pl.ds(pl.multiple_of(q * slice_width, slice_width), slice_width)],
            dst_ref=xc_ref.at[pl.ds(pl.multiple_of((p * nt + b) * rows, rows), rows), :],
            send_sem=p_send.at[b, r - 1], recv_sem=p_recv.at[b, r - 1],
            device_id={"dp": q // nc, "ctx": q % nc}, device_id_type=MESH,
        )

    def keep_copy(b, source):
        return pltpu.make_async_copy(
            source.at[:, pl.ds(pl.multiple_of(p * slice_width, slice_width), slice_width)],
            xc_ref.at[pl.ds(pl.multiple_of((p * nt + b) * rows, rows), rows), :],
            local_sem.at[3 + b],
        )

    def to_plane(b, source):
        for r in range(1, plane):
            plane_copy(b, r, source).start()
        keep_copy(b, source).start()

    def wide_at(r, q):
        return wide_ref.at[(t + nt - r) % nt, pl.ds(pl.multiple_of(q * piece, piece), piece), :]

    def fan_copy(r, j):
        hh = (h + j) % half
        return pltpu.make_async_remote_copy(
            src_ref=wide_at(r, p), dst_ref=wide_at(r, p),
            send_sem=f_send.at[r - 1, j - 1], recv_sem=f_recv.at[r - 1, j - 1],
            device_id={"dp": (hh // nc) * 2 + core, "ctx": hh % nc}, device_id_type=MESH,
        )

    def sibling_copy(r, j):
        hh = (h + half - j) % half
        q = ((hh // nc) * 2 + core) * nc + hh % nc
        return pltpu.make_async_remote_copy(
            src_ref=wide_at(r, q), dst_ref=wide_at(r, q),
            send_sem=s_send.at[r - 1, j], recv_sem=s_recv.at[r - 1, j],
            device_id={"dp": d + 1 - 2 * core}, device_id_type=MESH,
        )

    start_x(1)
    for r in range(1, nt):
        for which in (0, 1):
            w_copy(which, r).start()
    own = [
        pltpu.make_async_copy(x_ref, x_rows(t), local_sem.at[0]),
        pltpu.make_async_copy(
            kw_ref.at[pl.ds(pl.multiple_of(t * chunk, chunk), chunk), :],
            wide_ref.at[t, :, pl.ds(0, kv)], local_sem.at[1],
        ),
        pltpu.make_async_copy(
            vw_ref.at[pl.ds(pl.multiple_of(t * chunk, chunk), chunk), :],
            wide_ref.at[t, :, pl.ds(kv, kv)], local_sem.at[2],
        ),
    ]
    to_plane(t, x_ref)
    for copy in own:
        copy.start()
    for s in range(1, nt):
        for way in (0, 1):
            b = t - s if way == 0 else t + s

            @pl.when((b >= 0) & (b < nt))
            def _():
                x_copy(way, s, x_ref, b, (t + 1) % nt).wait_recv()

        if s < nt - 1:
            start_x(s + 1)
        for way in (0, 1):
            b = t - s if way == 0 else t + s

            @pl.when((b >= 0) & (b < nt))
            def _():
                to_plane(b, x_rows(b))

        for which in (0, 1):
            w_copy(which, s).wait_recv()
        for j in range(1, half):
            fan_copy(s, j).start()
        sibling_copy(s, 0).start()
    for s in range(1, nt):
        for j in range(1, half):
            fan_copy(s, j).wait_recv()
            sibling_copy(s, j).start()
    for s in range(1, nt):
        for way, ok, b, target in sends(s):
            @pl.when(ok)
            def _():
                x_copy(way, s, x_ref, b, target).wait_send()
        for which in (0, 1):
            w_copy(which, s).wait_send()
        for j in range(1, half):
            fan_copy(s, j).wait_send()
        for j in range(half):
            sibling_copy(s, j).wait()
    for b in range(nt):
        for r in range(1, plane):
            plane_copy(b, r, x_ref).wait()
        keep_copy(b, x_ref).wait()
    for copy in own:
        copy.wait()


def exchange_inputs(x, key_weight, value_weight):
    nt, nd, nc = lax.axis_size("tensor"), lax.axis_size("dp"), lax.axis_size("ctx")
    plane = nd * nc
    rows, width = x.shape
    kv = key_weight.shape[1]
    dma = pltpu.SemaphoreType.DMA
    return pl.pallas_call(
        functools.partial(exchange_kernel, nt, nd, nc),
        out_shape=(
            jax.ShapeDtypeStruct((nt * rows, width), x.dtype),
            jax.ShapeDtypeStruct((plane * nt * rows, width // plane), x.dtype),
            jax.ShapeDtypeStruct((nt, width // nt, 2 * kv), x.dtype),
        ),
        in_specs=[pl.BlockSpec(memory_space=pltpu.HBM)] * 3,
        out_specs=[pl.BlockSpec(memory_space=pltpu.HBM)] * 3,
        scratch_shapes=[
            dma((2, nt - 1)), dma((2, nt - 1)), dma((2, nt - 1)), dma((2, nt - 1)),
            dma((nt, plane - 1)), dma((nt, plane - 1)),
            dma((nt - 1, plane // 2 - 1)), dma((nt - 1, plane // 2 - 1)),
            dma((nt - 1, plane // 2)), dma((nt - 1, plane // 2)),
            dma((3 + nt,)),
        ],
        compiler_params=pltpu.CompilerParams(collective_id=0, has_side_effects=True),
    )(x, key_weight, value_weight)


def per_device(
    layer_input,
    queries,
    forward_output,
    attention_output_gradient,
    key_weight,
    value_projection_weight,
    segment,
    block_table,
    block_owner,
):
    softmax_scale = 1.0 / math.sqrt(HEAD_SIZE)
    local_rows = queries.shape[1]
    kv_local = key_weight.shape[1] // HEAD_SIZE
    q_local = queries.shape[2] // HEAD_SIZE
    queries_per_group = q_local // kv_local
    kv_width = kv_local * HEAD_SIZE
    gathered, plane_input, wide_weight = exchange_inputs(
        layer_input[0], key_weight, value_projection_weight
    )
    projected_keys = jnp.dot(gathered, key_weight, preferred_element_type=jnp.float32)
    projected_values = jnp.dot(
        gathered, value_projection_weight, preferred_element_type=jnp.float32
    )
    kv_rows = jnp.concatenate([projected_keys, projected_values], axis=1).astype(jnp.bfloat16)
    owner_row = block_owner[0]
    segments_row = segment[0]
    table_row = block_table[0]
    blocks_here = local_rows // BLK
    ctx_index = lax.axis_index("ctx")
    own_blocks = lax.dynamic_slice_in_dim(owner_row, ctx_index * blocks_here, blocks_here)
    offsets = jnp.arange(BLK, dtype=jnp.int32)
    query_pos = (own_blocks[:, None] * BLK + offsets[None, :]).reshape(-1)
    query_seg = jnp.take(segments_row, query_pos)
    own_table = jnp.take(table_row, own_blocks, axis=0)
    query_heads = queries[0].reshape(local_rows, kv_local, queries_per_group, HEAD_SIZE)
    grad_heads = attention_output_gradient[0].reshape(
        local_rows, kv_local, queries_per_group, HEAD_SIZE
    )
    saved_heads = forward_output[0].reshape(local_rows, kv_local, queries_per_group, HEAD_SIZE)
    correction = jnp.sum(grad_heads.astype(jnp.float32) * saved_heads.astype(jnp.float32), axis=-1)
    correction = correction.transpose(1, 2, 0)

    def allowed_for(leading_row, row_count):
        key_blocks = lax.dynamic_slice_in_dim(owner_row, leading_row // BLK, row_count // BLK)
        key_pos = (key_blocks[:, None] * BLK + offsets[None, :]).reshape(-1)
        key_seg = jnp.take(segments_row, key_pos)
        table_part = jnp.take(own_table, key_blocks, axis=1) == 1
        table_full = jnp.broadcast_to(
            table_part[:, None, :, None], (blocks_here, BLK, row_count // BLK, BLK)
        )
        table_full = table_full.reshape(local_rows, row_count)
        same_tree = (key_seg[None, :] == 0) | (key_seg[None, :] == query_seg[:, None])
        return table_full & (key_pos[None, :] <= query_pos[:, None]) & same_tree

    def block_scores(block_rows, leading_row):
        row_count = block_rows.shape[0]
        block_keys = block_rows[:, :kv_width].reshape(row_count, kv_local, HEAD_SIZE)
        block_values = block_rows[:, kv_width:].reshape(row_count, kv_local, HEAD_SIZE)
        raw_scores = (
            jnp.einsum(
                "qhgd,khd->hgqk", query_heads, block_keys, preferred_element_type=jnp.float32
            )
            * softmax_scale
        )
        allowed = allowed_for(leading_row, row_count)
        return (jnp.where(allowed[None, None], raw_scores, -jnp.inf), block_keys, block_values)

    def stats_block(carried, block_rows, leading_row):
        running_max, running_sum = carried
        scores = block_scores(block_rows, leading_row)[0]
        new_max = jnp.maximum(running_max, jnp.max(scores, axis=-1))
        running_sum = running_sum * jnp.exp(running_max - new_max) + jnp.sum(
            jnp.exp(scores - new_max[..., None]), axis=-1
        )
        return (new_max, running_sum)

    def grads_block(carried, block_rows, leading_row, log_norm):
        query_sum, keyval_sum = carried
        row_count = block_rows.shape[0]
        scores, block_keys, block_values = block_scores(block_rows, leading_row)
        probabilities = jnp.exp(scores - log_norm[..., None])
        probs_low = probabilities.astype(jnp.bfloat16)
        value_gradient_rows = jnp.einsum(
            "hgqk,qhgd->khd", probs_low, grad_heads, preferred_element_type=jnp.float32
        )
        prob_grads = jnp.einsum(
            "qhgd,khd->hgqk", grad_heads, block_values, preferred_element_type=jnp.float32
        )
        score_low = (probabilities * (prob_grads - correction[..., None])).astype(jnp.bfloat16)
        query_sum = query_sum + jnp.einsum(
            "hgqk,khd->qhgd", score_low, block_keys, preferred_element_type=jnp.float32
        )
        key_gradient_rows = (
            jnp.einsum("hgqk,qhgd->khd", score_low, query_heads, preferred_element_type=jnp.float32)
            * softmax_scale
        )
        update = jnp.concatenate(
            [
                key_gradient_rows.reshape(row_count, kv_width),
                value_gradient_rows.reshape(row_count, kv_width),
            ],
            axis=1,
        )
        keyval_sum = lax.dynamic_update_slice_in_dim(keyval_sum, update, leading_row, 0)
        return (query_sum, keyval_sum)

    def over_blocks(block_step, carried, shard_part):
        row_count = shard_part.shape[0]
        block_size = math.gcd(row_count, max(512, local_rows))
        block_count = row_count // block_size
        pieces = shard_part.reshape(block_count, block_size, shard_part.shape[1])
        starts = block_size * jnp.arange(block_count, dtype=jnp.int32)

        def one_block(state_in, scan_item):
            block_rows, block_start = scan_item
            result = block_step(state_in, block_rows, block_start)
            return (result, None)

        carried, _ = lax.scan(one_block, carried, (pieces, starts))
        return carried

    stats_init = (
        jnp.full((kv_local, queries_per_group, local_rows), -1e30, jnp.float32),
        jnp.zeros((kv_local, queries_per_group, local_rows), jnp.float32),
    )
    seq_rows = local_rows * lax.axis_size("ctx")
    grads_init = (
        jnp.zeros((local_rows, kv_local, queries_per_group, HEAD_SIZE), jnp.float32),
        jnp.zeros((seq_rows, 2 * kv_width), jnp.float32),
    )
    running_max, running_sum = over_blocks(
        stats_block, stats_init, lax.all_gather(kv_rows, "ctx", axis=0, tiled=True)
    )
    log_norm = running_max + jnp.log(running_sum)

    def grads_fold(carried, shard_part):
        return over_blocks(
            lambda state, rows_in, start_in: grads_block(state, rows_in, start_in, log_norm),
            carried,
            shard_part,
        )

    query_sum, keyval_sum = grads_fold(
        grads_init, lax.all_gather(kv_rows, "ctx", axis=0, tiled=True)
    )
    own_grads = lax.psum_scatter(keyval_sum, "ctx", scatter_dimension=0, tiled=True).astype(
        jnp.bfloat16
    )
    query_grad = (
        (query_sum * softmax_scale).astype(jnp.bfloat16).reshape(1, local_rows, q_local * HEAD_SIZE)
    )
    kv_all = lax.all_gather(own_grads, "tensor", axis=0)
    kv_plane = lax.all_gather(own_grads, ("dp", "ctx"), axis=0, tiled=True)
    width_part = lax.dot_general(
        kv_all, wide_weight, (((0, 2), (0, 2)), ((), ())), preferred_element_type=jnp.float32
    ).astype(jnp.bfloat16)
    input_grad = lax.all_to_all(width_part, "tensor", split_axis=0, concat_axis=1, tiled=True)[None]
    weight_sum = lax.dot_general(
        plane_input, kv_plane, (((0,), (0,)), ((), ())), preferred_element_type=jnp.float32
    )
    key_weight_grad = weight_sum[:, :kv_width].astype(jnp.bfloat16)
    value_weight_grad = weight_sum[:, kv_width:].astype(jnp.bfloat16)
    return (query_grad, input_grad, key_weight_grad, value_weight_grad)


def solution(mesh):
    in_specs = (
        P("dp", ("ctx", "tensor"), None),
        P("dp", "ctx", "tensor"),
        P("dp", "ctx", "tensor"),
        P("dp", "ctx", "tensor"),
        P(None, "tensor"),
        P(None, "tensor"),
        P("dp", None),
        P("dp", None, None),
        P("dp", None),
    )
    out_specs = (
        P("dp", "ctx", "tensor"),
        P("dp", ("ctx", "tensor"), None),
        P(("dp", "ctx"), "tensor"),
        P(("dp", "ctx"), "tensor"),
    )
    return jax.shard_map(
        per_device, mesh=mesh, in_specs=in_specs, out_specs=out_specs, check_vma=False
    )
```

```python
import functools
import math

import jax
import jax.numpy as jnp
from jax import lax
from jax.experimental import pallas as pl
from jax.experimental.pallas import tpu as pltpu
from jax.sharding import PartitionSpec as P

HEAD_SIZE = 128
BLK = 128

MESH = pl.DeviceIdType.MESH


def exchange_kernel(
    nt, nd, nc, x_ref, kw_ref, vw_ref, g_ref, xc4_ref, wide_ref,
    x_send, x_recv, w_send, w_recv, p_send, p_recv, f_send, f_recv, s_send, s_recv, local_sem, x_own, w_own, keep_own,
):
    t = lax.axis_index("tensor")
    d = lax.axis_index("dp")
    c = lax.axis_index("ctx")
    plane = nd * nc
    half = plane // 2
    p = d * nc + c
    h = (d // 2) * nc + c
    core = d % 2
    rows, width = x_ref.shape
    kv = kw_ref.shape[1]
    chunk = width // nt
    piece = chunk // plane
    slice_width = width // plane

    xc_ref = xc4_ref
    kept_ref = xc4_ref.at[p]

    barrier = pltpu.get_barrier_semaphore()
    for r in range(1, nt):
        pl.semaphore_signal(
            barrier, inc=1, device_id={"tensor": (t + r) % nt}, device_id_type=MESH
        )
    for r in range(1, plane):
        q = (p + r) % plane
        pl.semaphore_signal(
            barrier, inc=1, device_id={"dp": q // nc, "ctx": q % nc}, device_id_type=MESH
        )
    pl.semaphore_wait(barrier, nt - 1 + plane - 1)

    def x_rows(b):
        return g_ref.at[pl.ds(pl.multiple_of(b * rows, rows), rows), :]

    def x_copy(way, s, source, b, target):
        return pltpu.make_async_remote_copy(
            src_ref=source, dst_ref=x_rows(b), send_sem=x_send.at[way, s - 1],
            recv_sem=x_recv.at[way, s - 1], device_id={"tensor": target}, device_id_type=MESH,
        )

    def sends(s):
        for way in (0, 1):
            step = 1 if way == 0 else -1
            b = t - step * (s - 1)
            target = t + step
            ok = (target >= 0) & (target < nt) & (b >= 0) & (b < nt)
            yield way, ok, b, target

    def start_x(s):
        for way, ok, b, target in sends(s):
            @pl.when(ok)
            def _():
                x_copy(way, s, x_ref if s == 1 else x_rows(b), b, target).start()

    def w_copy(which, r):
        other = (t + r) % nt
        source = (kw_ref, vw_ref)[which].at[
            pl.ds(pl.multiple_of(other * chunk + p * piece, piece), piece), :
        ]
        return pltpu.make_async_remote_copy(
            src_ref=source,
            dst_ref=wide_ref.at[
                t, pl.ds(pl.multiple_of(p * piece, piece), piece), pl.ds(which * kv, kv)
            ],
            send_sem=w_send.at[which, r - 1], recv_sem=w_recv.at[which, r - 1],
            device_id={"tensor": other}, device_id_type=MESH,
        )

    def plane_copy(b, r, source):
        q = (p + r) % plane
        return pltpu.make_async_remote_copy(
            src_ref=source.at[:, pl.ds(pl.multiple_of(q * slice_width, slice_width), slice_width)],
            dst_ref=xc_ref.at[p, b],
            send_sem=p_send.at[b, r - 1], recv_sem=p_recv.at[b, r - 1],
            device_id={"dp": q // nc, "ctx": q % nc}, device_id_type=MESH,
        )

    def keep_copy(b, source):
        return pltpu.make_async_copy(
            source.at[:, pl.ds(pl.multiple_of(p * slice_width, slice_width), slice_width)],
            keep_own.at[b], local_sem.at[3 + b],
        )

    def to_plane(b, source):
        for r in range(1, plane):
            plane_copy(b, r, source).start()
        keep_copy(b, source).start()

    def wide_at(r, q):
        return wide_ref.at[(t + nt - r) % nt, pl.ds(pl.multiple_of(q * piece, piece), piece), :]

    def fan_copy(r, j):
        hh = (h + j) % half
        return pltpu.make_async_remote_copy(
            src_ref=wide_at(r, p), dst_ref=wide_at(r, p),
            send_sem=f_send.at[r - 1, j - 1], recv_sem=f_recv.at[r - 1, j - 1],
            device_id={"dp": (hh // nc) * 2 + core, "ctx": hh % nc}, device_id_type=MESH,
        )

    def sibling_copy(r, j):
        hh = (h + half - j) % half
        q = ((hh // nc) * 2 + core) * nc + hh % nc
        return pltpu.make_async_remote_copy(
            src_ref=wide_at(r, q), dst_ref=wide_at(r, q),
            send_sem=s_send.at[r - 1, j], recv_sem=s_recv.at[r - 1, j],
            device_id={"dp": d + 1 - 2 * core}, device_id_type=MESH,
        )

    for r in range(1, nt):
        for which in (0, 1):
            w_copy(which, r).start()
    start_x(1)
    own_chunk = pl.ds(pl.multiple_of(t * chunk, chunk), chunk)
    loads = [
        pltpu.make_async_copy(x_ref, x_own, local_sem.at[0]),
        pltpu.make_async_copy(kw_ref.at[own_chunk, :], w_own.at[:, pl.ds(0, kv)], local_sem.at[1]),
        pltpu.make_async_copy(vw_ref.at[own_chunk, :], w_own.at[:, pl.ds(kv, kv)], local_sem.at[2]),
    ]
    own = [
        pltpu.make_async_copy(x_own, x_rows(t), local_sem.at[0]),
        pltpu.make_async_copy(w_own, wide_ref.at[t], local_sem.at[1]),
    ]
    to_plane(t, x_ref)
    for copy in loads:
        copy.start()
    for copy in loads:
        copy.wait()
    for copy in own:
        copy.start()
    for s in range(1, nt):
        for which in (0, 1):
            w_copy(which, s).wait_recv()
        for j in range(1, half):
            fan_copy(s, j).start()
        sibling_copy(s, 0).start()
    for s in range(1, nt):
        for way in (0, 1):
            b = t - s if way == 0 else t + s

            @pl.when((b >= 0) & (b < nt))
            def _():
                x_copy(way, s, x_ref, b, (t + 1) % nt).wait_recv()

        if s < nt - 1:
            start_x(s + 1)
        for way in (0, 1):
            b = t - s if way == 0 else t + s

            @pl.when((b >= 0) & (b < nt))
            def _():
                to_plane(b, x_rows(b))

        if s == nt - 2:
            for r in range(1, nt):
                for j in range(1, half):
                    fan_copy(r, j).wait_recv()
                    sibling_copy(r, j).start()
    for s in range(1, nt):
        for way, ok, b, target in sends(s):
            @pl.when(ok)
            def _():
                x_copy(way, s, x_ref, b, target).wait_send()
        for which in (0, 1):
            w_copy(which, s).wait_send()
        for j in range(1, half):
            fan_copy(s, j).wait_send()
        for j in range(half):
            sibling_copy(s, j).wait()
    for b in range(nt):
        for r in range(1, plane):
            plane_copy(b, r, x_ref).wait()
    for b in range(nt):
        keep_copy(b, x_ref).wait()
    keep = pltpu.make_async_copy(
        keep_own, kept_ref, local_sem.at[2]
    )
    keep.start()
    for copy in own:
        copy.wait()
    keep.wait()


def exchange_inputs(x, key_weight, value_weight):
    nt, nd, nc = lax.axis_size("tensor"), lax.axis_size("dp"), lax.axis_size("ctx")
    plane = nd * nc
    rows, width = x.shape
    kv = key_weight.shape[1]
    dma = pltpu.SemaphoreType.DMA
    return pl.pallas_call(
        functools.partial(exchange_kernel, nt, nd, nc),
        out_shape=(
            jax.ShapeDtypeStruct((nt * rows, width), x.dtype),
            jax.ShapeDtypeStruct((plane, nt, rows, width // plane), x.dtype),
            jax.ShapeDtypeStruct((nt, width // nt, 2 * kv), x.dtype),
        ),
        in_specs=[pl.BlockSpec(memory_space=pltpu.HBM)] * 3,
        out_specs=[pl.BlockSpec(memory_space=pltpu.HBM)] * 3,
        scratch_shapes=[
            dma((2, nt - 1)), dma((2, nt - 1)), dma((2, nt - 1)), dma((2, nt - 1)),
            dma((nt, plane - 1)), dma((nt, plane - 1)),
            dma((nt - 1, plane // 2 - 1)), dma((nt - 1, plane // 2 - 1)),
            dma((nt - 1, plane // 2)), dma((nt - 1, plane // 2)),
            dma((3 + nt,)),
            pltpu.VMEM((rows, width), x.dtype),
            pltpu.VMEM((width // nt, 2 * kv), x.dtype),
            pltpu.VMEM((nt, rows, width // plane), x.dtype),
        ],
        compiler_params=pltpu.CompilerParams(collective_id=0, has_side_effects=True),
    )(x, key_weight, value_weight)


def finish_kernel(
    nt, nd, nc, sum_ref, wide_ref, xc_ref, dx_ref, dk_ref, dv_ref,
    part, kz, kp, wide, xc, dx_send,
    c_send, c_recv, z_send, z_recv, p_send, p_recv, d_send, d_recv, local_sem,
):
    t = lax.axis_index("tensor")
    d = lax.axis_index("dp")
    c = lax.axis_index("ctx")
    plane = nd * nc
    p = d * nc + c
    group_rows = kz.shape[1]
    rows, chunk = dx_send.shape[1:]
    kv = dk_ref.shape[1]

    load_wide = pltpu.make_async_copy(wide_ref, wide, local_sem.at[0])
    load_xc = pltpu.make_async_copy(xc_ref, xc, local_sem.at[1])
    load_wide.start()
    load_xc.start()
    barrier = pltpu.get_barrier_semaphore()
    for r in range(1, nt):
        pl.semaphore_signal(
            barrier, inc=1, device_id={"tensor": (t + r) % nt}, device_id_type=MESH
        )
    for r in range(1, plane):
        q = (p + r) % plane
        pl.semaphore_signal(
            barrier, inc=1, device_id={"dp": q // nc, "ctx": q % nc}, device_id_type=MESH
        )
    pl.semaphore_wait(barrier, nt - 1 + plane - 1)

    def block(i):
        return pl.ds(pl.multiple_of(i * group_rows, group_rows), group_rows)

    def part_copy(j):
        other = (c + j) % nc
        return pltpu.make_async_remote_copy(
            src_ref=sum_ref.at[block(other), :], dst_ref=part.at[j - 1],
            send_sem=c_send.at[j - 1], recv_sem=c_recv.at[j - 1],
            device_id={"ctx": other}, device_id_type=MESH,
        )

    def z_copy(r):
        return pltpu.make_async_remote_copy(
            src_ref=kz.at[t], dst_ref=kz.at[t], send_sem=z_send.at[r - 1],
            recv_sem=z_recv.at[r - 1], device_id={"tensor": (t + r) % nt}, device_id_type=MESH,
        )

    def p_copy(r):
        q = (p + r) % plane
        return pltpu.make_async_remote_copy(
            src_ref=kz.at[t], dst_ref=kp.at[block(p), :], send_sem=p_send.at[r - 1],
            recv_sem=p_recv.at[r - 1], device_id={"dp": q // nc, "ctx": q % nc},
            device_id_type=MESH,
        )

    def dx_part(r):
        other = (t + r) % nt
        return pltpu.make_async_remote_copy(
            src_ref=dx_send.at[other],
            dst_ref=dx_ref.at[:, pl.ds(pl.multiple_of(t * chunk, chunk), chunk)],
            send_sem=d_send.at[r - 1], recv_sem=d_recv.at[r - 1],
            device_id={"tensor": other}, device_id_type=MESH,
        )

    for j in range(1, nc):
        part_copy(j).start()
    for j in range(1, nc):
        part_copy(j).wait_recv()
    total = sum_ref[block(c), :]
    for j in range(1, nc):
        total = total + part[j - 1]
    total = total.astype(jnp.bfloat16)
    kz[t] = total
    kp[block(p), :] = total
    for r in range(1, nt):
        z_copy(r).start()
    for r in range(1, plane):
        p_copy(r).start()
    load_wide.wait()
    for r in range(1, nt):
        z_copy(r).wait_recv()
    tile = 256

    @pl.loop(0, chunk // tile)
    def _(n):
        columns = pl.ds(pl.multiple_of(n * tile, tile), tile)
        out = None
        for b in range(nt):
            term = lax.dot_general(
                kz[b], wide[b, columns, :], (((1,), (1,)), ((), ())),
                preferred_element_type=jnp.float32,
            )
            out = term if out is None else out + term
        dx_send[:, :, columns] = out.astype(jnp.bfloat16).reshape(nt, rows, tile)

    for r in range(1, nt):
        dx_part(r).start()
    keep = pltpu.make_async_copy(
        dx_send.at[t], dx_ref.at[:, pl.ds(pl.multiple_of(t * chunk, chunk), chunk)],
        local_sem.at[2],
    )
    keep.start()
    load_xc.wait()
    for r in range(1, plane):
        p_copy(r).wait_recv()

    @pl.loop(0, dk_ref.shape[0] // tile)
    def _(m):
        columns = pl.ds(pl.multiple_of(m * tile, tile), tile)
        out = lax.dot_general(
            xc[:, columns], kp[...], (((0,), (0,)), ((), ())),
            preferred_element_type=jnp.float32,
        )
        dk_ref[columns, :] = out[:, :kv].astype(jnp.bfloat16)
        dv_ref[columns, :] = out[:, kv:].astype(jnp.bfloat16)

    for j in range(1, nc):
        part_copy(j).wait_send()
    for r in range(1, nt):
        z_copy(r).wait_send()
        dx_part(r).wait()
    for r in range(1, plane):
        p_copy(r).wait_send()
    keep.wait()


def finish_grads(keyval_sum, wide_weight, plane_input):
    nt, nd, nc = lax.axis_size("tensor"), lax.axis_size("dp"), lax.axis_size("ctx")
    plane = nd * nc
    seq_rows, kv2 = keyval_sum.shape
    group_rows = seq_rows // nc
    chunk = wide_weight.shape[1]
    slice_width = plane_input.shape[1]
    low = plane_input.dtype
    dma = pltpu.SemaphoreType.DMA
    hbm = pl.BlockSpec(memory_space=pltpu.HBM)
    vmem = pl.BlockSpec(memory_space=pltpu.VMEM)
    return pl.pallas_call(
        functools.partial(finish_kernel, nt, nd, nc),
        out_shape=(
            jax.ShapeDtypeStruct((group_rows // nt, chunk * nt), low),
            jax.ShapeDtypeStruct((slice_width, kv2 // 2), low),
            jax.ShapeDtypeStruct((slice_width, kv2 // 2), low),
        ),
        in_specs=[vmem, hbm, hbm],
        out_specs=[hbm, vmem, vmem],
        scratch_shapes=[
            pltpu.VMEM((nc - 1, group_rows, kv2), jnp.float32),
            pltpu.VMEM((nt, group_rows, kv2), low),
            pltpu.VMEM((plane * group_rows, kv2), low),
            pltpu.VMEM(wide_weight.shape, low),
            pltpu.VMEM(plane_input.shape, low),
            pltpu.VMEM((nt, group_rows // nt, chunk), low),
            dma((nc - 1,)), dma((nc - 1,)), dma((nt - 1,)), dma((nt - 1,)),
            dma((plane - 1,)), dma((plane - 1,)), dma((nt - 1,)), dma((nt - 1,)), dma((3,)),
        ],
        compiler_params=pltpu.CompilerParams(
            collective_id=1, has_side_effects=True, vmem_limit_bytes=56 << 20
        ),
    )(keyval_sum, wide_weight, plane_input)


def per_device(
    layer_input,
    queries,
    forward_output,
    attention_output_gradient,
    key_weight,
    value_projection_weight,
    segment,
    block_table,
    block_owner,
):
    softmax_scale = 1.0 / math.sqrt(HEAD_SIZE)
    local_rows = queries.shape[1]
    kv_local = key_weight.shape[1] // HEAD_SIZE
    q_local = queries.shape[2] // HEAD_SIZE
    queries_per_group = q_local // kv_local
    kv_width = kv_local * HEAD_SIZE
    gathered, plane_input, wide_weight = exchange_inputs(
        layer_input[0], key_weight, value_projection_weight
    )
    plane_input = plane_input.reshape(-1, plane_input.shape[3])
    projected_keys = jnp.dot(gathered, key_weight, preferred_element_type=jnp.float32)
    projected_values = jnp.dot(
        gathered, value_projection_weight, preferred_element_type=jnp.float32
    )
    kv_rows = jnp.concatenate([projected_keys, projected_values], axis=1).astype(jnp.bfloat16)
    owner_row = block_owner[0]
    segments_row = segment[0]
    table_row = block_table[0]
    blocks_here = local_rows // BLK
    ctx_index = lax.axis_index("ctx")
    own_blocks = lax.dynamic_slice_in_dim(owner_row, ctx_index * blocks_here, blocks_here)
    offsets = jnp.arange(BLK, dtype=jnp.int32)
    query_pos = (own_blocks[:, None] * BLK + offsets[None, :]).reshape(-1)
    query_seg = jnp.take(segments_row, query_pos)
    own_table = jnp.take(table_row, own_blocks, axis=0)
    query_heads = queries[0].reshape(local_rows, kv_local, queries_per_group, HEAD_SIZE)
    grad_heads = attention_output_gradient[0].reshape(
        local_rows, kv_local, queries_per_group, HEAD_SIZE
    )
    saved_heads = forward_output[0].reshape(local_rows, kv_local, queries_per_group, HEAD_SIZE)
    correction = jnp.sum(grad_heads.astype(jnp.float32) * saved_heads.astype(jnp.float32), axis=-1)
    correction = correction.transpose(1, 2, 0)

    def allowed_for(leading_row, row_count):
        key_blocks = lax.dynamic_slice_in_dim(owner_row, leading_row // BLK, row_count // BLK)
        key_pos = (key_blocks[:, None] * BLK + offsets[None, :]).reshape(-1)
        key_seg = jnp.take(segments_row, key_pos)
        table_part = jnp.take(own_table, key_blocks, axis=1) == 1
        table_full = jnp.broadcast_to(
            table_part[:, None, :, None], (blocks_here, BLK, row_count // BLK, BLK)
        )
        table_full = table_full.reshape(local_rows, row_count)
        same_tree = (key_seg[None, :] == 0) | (key_seg[None, :] == query_seg[:, None])
        return table_full & (key_pos[None, :] <= query_pos[:, None]) & same_tree

    def block_scores(block_rows, leading_row):
        row_count = block_rows.shape[0]
        block_keys = block_rows[:, :kv_width].reshape(row_count, kv_local, HEAD_SIZE)
        block_values = block_rows[:, kv_width:].reshape(row_count, kv_local, HEAD_SIZE)
        raw_scores = (
            jnp.einsum(
                "qhgd,khd->hgqk", query_heads, block_keys, preferred_element_type=jnp.float32
            )
            * softmax_scale
        )
        allowed = allowed_for(leading_row, row_count)
        return (jnp.where(allowed[None, None], raw_scores, -jnp.inf), block_keys, block_values)

    def stats_block(carried, block_rows, leading_row):
        running_max, running_sum = carried
        scores = block_scores(block_rows, leading_row)[0]
        new_max = jnp.maximum(running_max, jnp.max(scores, axis=-1))
        running_sum = running_sum * jnp.exp(running_max - new_max) + jnp.sum(
            jnp.exp(scores - new_max[..., None]), axis=-1
        )
        return (new_max, running_sum)

    def grads_block(carried, block_rows, leading_row, log_norm):
        query_sum, keyval_sum = carried
        row_count = block_rows.shape[0]
        scores, block_keys, block_values = block_scores(block_rows, leading_row)
        probabilities = jnp.exp(scores - log_norm[..., None])
        probs_low = probabilities.astype(jnp.bfloat16)
        value_gradient_rows = jnp.einsum(
            "hgqk,qhgd->khd", probs_low, grad_heads, preferred_element_type=jnp.float32
        )
        prob_grads = jnp.einsum(
            "qhgd,khd->hgqk", grad_heads, block_values, preferred_element_type=jnp.float32
        )
        score_low = (probabilities * (prob_grads - correction[..., None])).astype(jnp.bfloat16)
        query_sum = query_sum + jnp.einsum(
            "hgqk,khd->qhgd", score_low, block_keys, preferred_element_type=jnp.float32
        )
        key_gradient_rows = (
            jnp.einsum("hgqk,qhgd->khd", score_low, query_heads, preferred_element_type=jnp.float32)
            * softmax_scale
        )
        update = jnp.concatenate(
            [
                key_gradient_rows.reshape(row_count, kv_width),
                value_gradient_rows.reshape(row_count, kv_width),
            ],
            axis=1,
        )
        keyval_sum = lax.dynamic_update_slice_in_dim(keyval_sum, update, leading_row, 0)
        return (query_sum, keyval_sum)

    def over_blocks(block_step, carried, shard_part):
        row_count = shard_part.shape[0]
        block_size = math.gcd(row_count, max(512, local_rows))
        block_count = row_count // block_size
        pieces = shard_part.reshape(block_count, block_size, shard_part.shape[1])
        starts = block_size * jnp.arange(block_count, dtype=jnp.int32)

        def one_block(state_in, scan_item):
            block_rows, block_start = scan_item
            result = block_step(state_in, block_rows, block_start)
            return (result, None)

        carried, _ = lax.scan(one_block, carried, (pieces, starts))
        return carried

    stats_init = (
        jnp.full((kv_local, queries_per_group, local_rows), -1e30, jnp.float32),
        jnp.zeros((kv_local, queries_per_group, local_rows), jnp.float32),
    )
    seq_rows = local_rows * lax.axis_size("ctx")
    grads_init = (
        jnp.zeros((local_rows, kv_local, queries_per_group, HEAD_SIZE), jnp.float32),
        jnp.zeros((seq_rows, 2 * kv_width), jnp.float32),
    )
    running_max, running_sum = over_blocks(
        stats_block, stats_init, lax.all_gather(kv_rows, "ctx", axis=0, tiled=True)
    )
    log_norm = running_max + jnp.log(running_sum)

    def grads_fold(carried, shard_part):
        return over_blocks(
            lambda state, rows_in, start_in: grads_block(state, rows_in, start_in, log_norm),
            carried,
            shard_part,
        )

    query_sum, keyval_sum = grads_fold(
        grads_init, lax.all_gather(kv_rows, "ctx", axis=0, tiled=True)
    )
    query_grad = (
        (query_sum * softmax_scale).astype(jnp.bfloat16).reshape(1, local_rows, q_local * HEAD_SIZE)
    )
    input_grad, key_weight_grad, value_weight_grad = finish_grads(
        keyval_sum, wide_weight, plane_input
    )
    input_grad = input_grad[None]
    return (query_grad, input_grad, key_weight_grad, value_weight_grad)


def solution(mesh):
    in_specs = (
        P("dp", ("ctx", "tensor"), None),
        P("dp", "ctx", "tensor"),
        P("dp", "ctx", "tensor"),
        P("dp", "ctx", "tensor"),
        P(None, "tensor"),
        P(None, "tensor"),
        P("dp", None),
        P("dp", None, None),
        P("dp", None),
    )
    out_specs = (
        P("dp", "ctx", "tensor"),
        P("dp", ("ctx", "tensor"), None),
        P(("dp", "ctx"), "tensor"),
        P(("dp", "ctx"), "tensor"),
    )
    return jax.shard_map(
        per_device, mesh=mesh, in_specs=in_specs, out_specs=out_specs, check_vma=False
    )
```

```python
import functools
import math

import jax
import jax.numpy as jnp
from jax import lax
from jax.experimental import pallas as pl
from jax.experimental.pallas import tpu as pltpu
from jax.sharding import PartitionSpec as P

HEAD_SIZE = 128
BLK = 128

MESH = pl.DeviceIdType.MESH


def exchange_kernel(
    nt, nd, nc, x_ref, kw_ref, vw_ref, kv_ref, xc_ref, wide_ref,
    x_send, x_recv, w_send, w_recv, p_send, p_recv, f_send, f_recv, s_send, s_recv,
    k_send, k_recv, local_sem, g_ref, kw, vw, sums,
):
    t = lax.axis_index("tensor")
    d = lax.axis_index("dp")
    c = lax.axis_index("ctx")
    plane = nd * nc
    half = plane // 2
    p = d * nc + c
    h = (d // 2) * nc + c
    core = d % 2
    rows, width = x_ref.shape
    kv = kw_ref.shape[1]
    chunk = width // nt
    piece = chunk // plane
    slice_width = width // plane

    barrier = pltpu.get_barrier_semaphore()
    for r in range(1, nt):
        pl.semaphore_signal(
            barrier, inc=1, device_id={"tensor": (t + r) % nt}, device_id_type=MESH
        )
    for r in range(1, plane):
        q = (p + r) % plane
        pl.semaphore_signal(
            barrier, inc=1, device_id={"dp": q // nc, "ctx": q % nc}, device_id_type=MESH
        )
    pl.semaphore_wait(barrier, nt - 1 + plane - 1)

    def x_rows(b):
        return g_ref.at[pl.ds(pl.multiple_of(b * rows, rows), rows), :]

    def x_copy(way, s, source, b, target):
        return pltpu.make_async_remote_copy(
            src_ref=source, dst_ref=x_rows(b), send_sem=x_send.at[way, s - 1],
            recv_sem=x_recv.at[way, s - 1], device_id={"tensor": target}, device_id_type=MESH,
        )

    def sends(s):
        for way in (0, 1):
            step = 1 if way == 0 else -1
            b = t - step * (s - 1)
            target = t + step
            ok = (target >= 0) & (target < nt) & (b >= 0) & (b < nt)
            yield way, ok, b, target

    def start_x(s):
        for way, ok, b, target in sends(s):
            @pl.when(ok)
            def _():
                x_copy(way, s, x_ref if s == 1 else x_rows(b), b, target).start()

    def w_copy(which, r):
        other = (t + r) % nt
        source = (kw_ref, vw_ref)[which].at[
            pl.ds(pl.multiple_of(other * chunk + p * piece, piece), piece), :
        ]
        return pltpu.make_async_remote_copy(
            src_ref=source,
            dst_ref=wide_ref.at[
                t, pl.ds(pl.multiple_of(p * piece, piece), piece), pl.ds(which * kv, kv)
            ],
            send_sem=w_send.at[which, r - 1], recv_sem=w_recv.at[which, r - 1],
            device_id={"tensor": other}, device_id_type=MESH,
        )

    def plane_copy(b, r, source):
        q = (p + r) % plane
        return pltpu.make_async_remote_copy(
            src_ref=source.at[:, pl.ds(pl.multiple_of(q * slice_width, slice_width), slice_width)],
            dst_ref=xc_ref.at[p, b],
            send_sem=p_send.at[b, r - 1], recv_sem=p_recv.at[b, r - 1],
            device_id={"dp": q // nc, "ctx": q % nc}, device_id_type=MESH,
        )

    def keep_copy(b):
        return pltpu.make_async_copy(
            x_rows(b).at[:, pl.ds(pl.multiple_of(p * slice_width, slice_width), slice_width)],
            xc_ref.at[p, b], local_sem.at[3 + b],
        )

    def rows_of(i):
        return pl.ds(pl.multiple_of(i * nt * rows, nt * rows), nt * rows)

    def kv_copy(j):
        return pltpu.make_async_remote_copy(
            src_ref=kv_ref.at[rows_of(c), :], dst_ref=kv_ref.at[rows_of(c), :],
            send_sem=k_send.at[j - 1], recv_sem=k_recv.at[j - 1],
            device_id={"ctx": (c + j) % nc}, device_id_type=MESH,
        )

    def to_plane(b, source):
        for r in range(1, plane):
            plane_copy(b, r, source).start()

    def wide_at(r, q):
        return wide_ref.at[(t + nt - r) % nt, pl.ds(pl.multiple_of(q * piece, piece), piece), :]

    def fan_copy(r, j):
        hh = (h + j) % half
        return pltpu.make_async_remote_copy(
            src_ref=wide_at(r, p), dst_ref=wide_at(r, p),
            send_sem=f_send.at[r - 1, j - 1], recv_sem=f_recv.at[r - 1, j - 1],
            device_id={"dp": (hh // nc) * 2 + core, "ctx": hh % nc}, device_id_type=MESH,
        )

    def sibling_copy(r, j):
        hh = (h + half - j) % half
        q = ((hh // nc) * 2 + core) * nc + hh % nc
        return pltpu.make_async_remote_copy(
            src_ref=wide_at(r, q), dst_ref=wide_at(r, q),
            send_sem=s_send.at[r - 1, j], recv_sem=s_recv.at[r - 1, j],
            device_id={"dp": d + 1 - 2 * core}, device_id_type=MESH,
        )

    for r in range(1, nt):
        for which in (0, 1):
            w_copy(which, r).start()
    start_x(1)
    to_plane(t, x_ref)
    loads = [
        pltpu.make_async_copy(x_ref, x_rows(t), local_sem.at[0]),
        pltpu.make_async_copy(kw_ref, kw, local_sem.at[1]),
        pltpu.make_async_copy(vw_ref, vw, local_sem.at[2]),
    ]
    for copy in loads:
        copy.start()
    for copy in loads:
        copy.wait()
    keep_copy(t).start()
    own_chunk = pl.ds(pl.multiple_of(t * chunk, chunk), chunk)
    own = [
        pltpu.make_async_copy(
            kw.at[own_chunk, :], wide_ref.at[t, :, pl.ds(0, kv)], local_sem.at[1]
        ),
        pltpu.make_async_copy(
            vw.at[own_chunk, :], wide_ref.at[t, :, pl.ds(kv, kv)], local_sem.at[2]
        ),
    ]
    for copy in own:
        copy.start()
    for s in range(1, nt):
        for which in (0, 1):
            w_copy(which, s).wait_recv()
        for j in range(1, half):
            fan_copy(s, j).start()
        sibling_copy(s, 0).start()
    for s in range(1, nt):
        for way in (0, 1):
            b = t - s if way == 0 else t + s

            @pl.when((b >= 0) & (b < nt))
            def _():
                x_copy(way, s, x_ref, b, (t + 1) % nt).wait_recv()

        if s < nt - 1:
            start_x(s + 1)
        for way in (0, 1):
            b = t - s if way == 0 else t + s

            @pl.when((b >= 0) & (b < nt))
            def _():
                to_plane(b, x_rows(b))
                keep_copy(b).start()

        if s == nt - 2:
            for r in range(1, nt):
                for j in range(1, half):
                    fan_copy(r, j).wait_recv()
                    sibling_copy(r, j).start()
    sums[...] = jnp.zeros_like(sums)
    depth = min(1024, width)

    @pl.loop(0, width // depth)
    def _(i):
        part = pl.ds(pl.multiple_of(i * depth, depth), depth)
        left = g_ref[:, part]
        sums[:, :kv] += jnp.dot(left, kw[part, :], preferred_element_type=jnp.float32)
        sums[:, kv:] += jnp.dot(left, vw[part, :], preferred_element_type=jnp.float32)

    kv_ref[rows_of(c), :] = sums[...].astype(jnp.bfloat16)
    for j in range(1, nc):
        kv_copy(j).start()
    for j in range(1, nc):
        kv_copy(j).wait()
    for s in range(1, nt):
        for way, ok, b, target in sends(s):
            @pl.when(ok)
            def _():
                x_copy(way, s, x_ref, b, target).wait_send()
        for which in (0, 1):
            w_copy(which, s).wait_send()
        for j in range(1, half):
            fan_copy(s, j).wait_send()
        for j in range(half):
            sibling_copy(s, j).wait()
    for b in range(nt):
        for r in range(1, plane):
            plane_copy(b, r, x_ref).wait()
        keep_copy(b).wait()
    for copy in own:
        copy.wait()


def exchange_inputs(x, key_weight, value_weight):
    nt, nd, nc = lax.axis_size("tensor"), lax.axis_size("dp"), lax.axis_size("ctx")
    plane = nd * nc
    rows, width = x.shape
    kv = key_weight.shape[1]
    dma = pltpu.SemaphoreType.DMA
    return pl.pallas_call(
        functools.partial(exchange_kernel, nt, nd, nc),
        out_shape=(
            jax.ShapeDtypeStruct((nc * nt * rows, 2 * kv), x.dtype),
            jax.ShapeDtypeStruct((plane, nt, rows, width // plane), x.dtype),
            jax.ShapeDtypeStruct((nt, width // nt, 2 * kv), x.dtype),
        ),
        in_specs=[pl.BlockSpec(memory_space=pltpu.HBM)] * 3,
        out_specs=[
            pl.BlockSpec(memory_space=pltpu.VMEM),
            pl.BlockSpec(memory_space=pltpu.HBM),
            pl.BlockSpec(memory_space=pltpu.HBM),
        ],
        scratch_shapes=[
            dma((2, nt - 1)), dma((2, nt - 1)), dma((2, nt - 1)), dma((2, nt - 1)),
            dma((nt, plane - 1)), dma((nt, plane - 1)),
            dma((nt - 1, plane // 2 - 1)), dma((nt - 1, plane // 2 - 1)),
            dma((nt - 1, plane // 2)), dma((nt - 1, plane // 2)),
            dma((nc - 1,)), dma((nc - 1,)), dma((3 + nt,)),
            pltpu.VMEM((nt * rows, width), x.dtype),
            pltpu.VMEM((width, kv), x.dtype),
            pltpu.VMEM((width, kv), x.dtype),
            pltpu.VMEM((nt * rows, 2 * kv), jnp.float32),
        ],
        compiler_params=pltpu.CompilerParams(
            collective_id=0, has_side_effects=True, vmem_limit_bytes=48 << 20
        ),
    )(x, key_weight, value_weight)


def finish_kernel(
    nt, nd, nc, sum_ref, wide_ref, xc_ref, dx_ref, dw_ref,
    part, kz, kp, wide, xc, dx_send,
    c_send, c_recv, z_send, z_recv, p_send, p_recv, d_send, d_recv, local_sem,
):
    t = lax.axis_index("tensor")
    d = lax.axis_index("dp")
    c = lax.axis_index("ctx")
    plane = nd * nc
    p = d * nc + c
    group_rows = kz.shape[1]
    rows, chunk = dx_send.shape[1:]

    load_wide = pltpu.make_async_copy(wide_ref, wide, local_sem.at[0])
    load_xc = pltpu.make_async_copy(xc_ref, xc, local_sem.at[1])
    load_wide.start()
    load_xc.start()
    barrier = pltpu.get_barrier_semaphore()
    for r in range(1, nt):
        pl.semaphore_signal(
            barrier, inc=1, device_id={"tensor": (t + r) % nt}, device_id_type=MESH
        )
    for r in range(1, plane):
        q = (p + r) % plane
        pl.semaphore_signal(
            barrier, inc=1, device_id={"dp": q // nc, "ctx": q % nc}, device_id_type=MESH
        )
    pl.semaphore_wait(barrier, nt - 1 + plane - 1)

    def block(i):
        return pl.ds(pl.multiple_of(i * group_rows, group_rows), group_rows)

    def part_copy(j):
        other = (c + j) % nc
        return pltpu.make_async_remote_copy(
            src_ref=sum_ref.at[block(other), :], dst_ref=part.at[j - 1],
            send_sem=c_send.at[j - 1], recv_sem=c_recv.at[j - 1],
            device_id={"ctx": other}, device_id_type=MESH,
        )

    def z_copy(r):
        return pltpu.make_async_remote_copy(
            src_ref=kz.at[t], dst_ref=kz.at[t], send_sem=z_send.at[r - 1],
            recv_sem=z_recv.at[r - 1], device_id={"tensor": (t + r) % nt}, device_id_type=MESH,
        )

    def p_copy(r):
        q = (p + r) % plane
        return pltpu.make_async_remote_copy(
            src_ref=kz.at[t], dst_ref=kp.at[block(p), :], send_sem=p_send.at[r - 1],
            recv_sem=p_recv.at[r - 1], device_id={"dp": q // nc, "ctx": q % nc},
            device_id_type=MESH,
        )

    def dx_part(r):
        other = (t + r) % nt
        return pltpu.make_async_remote_copy(
            src_ref=dx_send.at[other],
            dst_ref=dx_ref.at[:, pl.ds(pl.multiple_of(t * chunk, chunk), chunk)],
            send_sem=d_send.at[r - 1], recv_sem=d_recv.at[r - 1],
            device_id={"tensor": other}, device_id_type=MESH,
        )

    for j in range(1, nc):
        part_copy(j).start()
    for j in range(1, nc):
        part_copy(j).wait_recv()
    total = sum_ref[block(c), :]
    for j in range(1, nc):
        total = total + part[j - 1]
    total = total.astype(jnp.bfloat16)
    kz[t] = total
    kp[block(p), :] = total
    for r in range(1, nt):
        z_copy(r).start()
    for r in range(1, plane):
        p_copy(r).start()
    load_wide.wait()
    for r in range(1, nt):
        z_copy(r).wait_recv()
    tile = 256

    @pl.loop(0, chunk // tile)
    def _(n):
        columns = pl.ds(pl.multiple_of(n * tile, tile), tile)
        out = None
        for b in range(nt):
            term = lax.dot_general(
                kz[b], wide[b, columns, :], (((1,), (1,)), ((), ())),
                preferred_element_type=jnp.float32,
            )
            out = term if out is None else out + term
        dx_send[:, :, columns] = out.astype(jnp.bfloat16).reshape(nt, rows, tile)

    for r in range(1, nt):
        dx_part(r).start()
    keep = pltpu.make_async_copy(
        dx_send.at[t], dx_ref.at[:, pl.ds(pl.multiple_of(t * chunk, chunk), chunk)],
        local_sem.at[2],
    )
    keep.start()
    load_xc.wait()
    for r in range(1, plane):
        p_copy(r).wait_recv()

    @pl.loop(0, dw_ref.shape[0] // tile)
    def _(m):
        columns = pl.ds(pl.multiple_of(m * tile, tile), tile)
        out = lax.dot_general(
            xc[:, columns], kp[...], (((0,), (0,)), ((), ())),
            preferred_element_type=jnp.float32,
        )
        dw_ref[columns, :] = out.astype(jnp.bfloat16)

    for j in range(1, nc):
        part_copy(j).wait_send()
    for r in range(1, nt):
        z_copy(r).wait_send()
        dx_part(r).wait()
    for r in range(1, plane):
        p_copy(r).wait_send()
    keep.wait()


def finish_grads(keyval_sum, wide_weight, plane_input):
    nt, nd, nc = lax.axis_size("tensor"), lax.axis_size("dp"), lax.axis_size("ctx")
    plane = nd * nc
    seq_rows, kv2 = keyval_sum.shape
    group_rows = seq_rows // nc
    chunk = wide_weight.shape[1]
    slice_width = plane_input.shape[1]
    low = plane_input.dtype
    dma = pltpu.SemaphoreType.DMA
    hbm = pl.BlockSpec(memory_space=pltpu.HBM)
    vmem = pl.BlockSpec(memory_space=pltpu.VMEM)
    return pl.pallas_call(
        functools.partial(finish_kernel, nt, nd, nc),
        out_shape=(
            jax.ShapeDtypeStruct((group_rows // nt, chunk * nt), low),
            jax.ShapeDtypeStruct((slice_width, kv2), low),
        ),
        in_specs=[vmem, hbm, hbm],
        out_specs=[hbm, vmem],
        scratch_shapes=[
            pltpu.VMEM((nc - 1, group_rows, kv2), jnp.float32),
            pltpu.VMEM((nt, group_rows, kv2), low),
            pltpu.VMEM((plane * group_rows, kv2), low),
            pltpu.VMEM(wide_weight.shape, low),
            pltpu.VMEM(plane_input.shape, low),
            pltpu.VMEM((nt, group_rows // nt, chunk), low),
            dma((nc - 1,)), dma((nc - 1,)), dma((nt - 1,)), dma((nt - 1,)),
            dma((plane - 1,)), dma((plane - 1,)), dma((nt - 1,)), dma((nt - 1,)), dma((3,)),
        ],
        compiler_params=pltpu.CompilerParams(
            collective_id=1, has_side_effects=True, vmem_limit_bytes=56 << 20
        ),
    )(keyval_sum, wide_weight, plane_input)


def per_device(
    layer_input,
    queries,
    forward_output,
    attention_output_gradient,
    key_weight,
    value_projection_weight,
    segment,
    block_table,
    block_owner,
):
    softmax_scale = 1.0 / math.sqrt(HEAD_SIZE)
    local_rows = queries.shape[1]
    kv_local = key_weight.shape[1] // HEAD_SIZE
    q_local = queries.shape[2] // HEAD_SIZE
    queries_per_group = q_local // kv_local
    kv_width = kv_local * HEAD_SIZE
    kv_full, plane_input, wide_weight = exchange_inputs(
        layer_input[0], key_weight, value_projection_weight
    )
    plane_input = plane_input.reshape(-1, plane_input.shape[3])
    owner_row = block_owner[0]
    segments_row = segment[0]
    table_row = block_table[0]
    blocks_here = local_rows // BLK
    ctx_index = lax.axis_index("ctx")
    own_blocks = lax.dynamic_slice_in_dim(owner_row, ctx_index * blocks_here, blocks_here)
    offsets = jnp.arange(BLK, dtype=jnp.int32)
    query_pos = (own_blocks[:, None] * BLK + offsets[None, :]).reshape(-1)
    block_ids = jnp.arange(owner_row.shape[0], dtype=jnp.int32)
    segment_blocks = segments_row.reshape(-1, BLK)

    def segments_of(blocks):
        chosen = (blocks[:, None] == block_ids[None, :])[:, :, None]
        return jnp.sum(jnp.where(chosen, segment_blocks[None], 0), axis=1).reshape(-1)

    query_seg = segments_of(own_blocks)
    own_chosen = (own_blocks[:, None] == block_ids[None, :])[:, :, None]
    own_table = jnp.sum(jnp.where(own_chosen, table_row[None], 0), axis=1)
    query_heads = queries[0].reshape(local_rows, kv_local, queries_per_group, HEAD_SIZE)
    grad_heads = attention_output_gradient[0].reshape(
        local_rows, kv_local, queries_per_group, HEAD_SIZE
    )
    saved_heads = forward_output[0].reshape(local_rows, kv_local, queries_per_group, HEAD_SIZE)
    correction = jnp.sum(grad_heads.astype(jnp.float32) * saved_heads.astype(jnp.float32), axis=-1)
    correction = correction.transpose(1, 2, 0)

    def allowed_for(leading_row, row_count):
        key_blocks = lax.dynamic_slice_in_dim(owner_row, leading_row // BLK, row_count // BLK)
        key_pos = (key_blocks[:, None] * BLK + offsets[None, :]).reshape(-1)
        key_seg = segments_of(key_blocks)
        key_chosen = (key_blocks[:, None] == block_ids[None, :])[None]
        table_part = jnp.sum(jnp.where(key_chosen, own_table[:, None, :], 0), axis=2) == 1
        table_full = jnp.broadcast_to(
            table_part[:, None, :, None], (blocks_here, BLK, row_count // BLK, BLK)
        )
        table_full = table_full.reshape(local_rows, row_count)
        same_tree = (key_seg[None, :] == 0) | (key_seg[None, :] == query_seg[:, None])
        return table_full & (key_pos[None, :] <= query_pos[:, None]) & same_tree

    def block_scores(block_rows, leading_row):
        row_count = block_rows.shape[0]
        block_keys = block_rows[:, :kv_width].reshape(row_count, kv_local, HEAD_SIZE)
        block_values = block_rows[:, kv_width:].reshape(row_count, kv_local, HEAD_SIZE)
        raw_scores = (
            jnp.einsum(
                "qhgd,khd->hgqk", query_heads, block_keys, preferred_element_type=jnp.float32
            )
            * softmax_scale
        )
        allowed = allowed_for(leading_row, row_count)
        return (jnp.where(allowed[None, None], raw_scores, -jnp.inf), block_keys, block_values)

    def stats_block(carried, block_rows, leading_row):
        running_max, running_sum = carried
        scores = block_scores(block_rows, leading_row)[0]
        new_max = jnp.maximum(running_max, jnp.max(scores, axis=-1))
        running_sum = running_sum * jnp.exp(running_max - new_max) + jnp.sum(
            jnp.exp(scores - new_max[..., None]), axis=-1
        )
        return (new_max, running_sum)

    def grads_block(carried, block_rows, leading_row, log_norm):
        query_sum, keyval_sum = carried
        row_count = block_rows.shape[0]
        scores, block_keys, block_values = block_scores(block_rows, leading_row)
        probabilities = jnp.exp(scores - log_norm[..., None])
        probs_low = probabilities.astype(jnp.bfloat16)
        value_gradient_rows = jnp.einsum(
            "hgqk,qhgd->khd", probs_low, grad_heads, preferred_element_type=jnp.float32
        )
        prob_grads = jnp.einsum(
            "qhgd,khd->hgqk", grad_heads, block_values, preferred_element_type=jnp.float32
        )
        score_low = (probabilities * (prob_grads - correction[..., None])).astype(jnp.bfloat16)
        query_sum = query_sum + jnp.einsum(
            "hgqk,khd->qhgd", score_low, block_keys, preferred_element_type=jnp.float32
        )
        key_gradient_rows = (
            jnp.einsum("hgqk,qhgd->khd", score_low, query_heads, preferred_element_type=jnp.float32)
            * softmax_scale
        )
        update = jnp.concatenate(
            [
                key_gradient_rows.reshape(row_count, kv_width),
                value_gradient_rows.reshape(row_count, kv_width),
            ],
            axis=1,
        )
        keyval_sum = lax.dynamic_update_slice_in_dim(keyval_sum, update, leading_row, 0)
        return (query_sum, keyval_sum)

    def over_blocks(block_step, carried, shard_part):
        row_count = shard_part.shape[0]
        block_size = math.gcd(row_count, max(512, local_rows))
        block_count = row_count // block_size
        pieces = shard_part.reshape(block_count, block_size, shard_part.shape[1])
        starts = block_size * jnp.arange(block_count, dtype=jnp.int32)

        def one_block(state_in, scan_item):
            block_rows, block_start = scan_item
            result = block_step(state_in, block_rows, block_start)
            return (result, None)

        carried, _ = lax.scan(one_block, carried, (pieces, starts))
        return carried

    stats_init = (
        jnp.full((kv_local, queries_per_group, local_rows), -1e30, jnp.float32),
        jnp.zeros((kv_local, queries_per_group, local_rows), jnp.float32),
    )
    seq_rows = local_rows * lax.axis_size("ctx")
    grads_init = (
        jnp.zeros((local_rows, kv_local, queries_per_group, HEAD_SIZE), jnp.float32),
        jnp.zeros((seq_rows, 2 * kv_width), jnp.float32),
    )
    running_max, running_sum = over_blocks(
        stats_block, stats_init, kv_full
    )
    log_norm = running_max + jnp.log(running_sum)

    def grads_fold(carried, shard_part):
        return over_blocks(
            lambda state, rows_in, start_in: grads_block(state, rows_in, start_in, log_norm),
            carried,
            shard_part,
        )

    query_sum, keyval_sum = grads_fold(
        grads_init, kv_full
    )
    query_grad = (
        (query_sum * softmax_scale).astype(jnp.bfloat16).reshape(1, local_rows, q_local * HEAD_SIZE)
    )
    input_grad, weight_grads = finish_grads(keyval_sum, wide_weight, plane_input)
    key_weight_grad = weight_grads[:, :kv_width]
    value_weight_grad = weight_grads[:, kv_width:]
    input_grad = input_grad[None]
    return (query_grad, input_grad, key_weight_grad, value_weight_grad)


def solution(mesh):
    in_specs = (
        P("dp", ("ctx", "tensor"), None),
        P("dp", "ctx", "tensor"),
        P("dp", "ctx", "tensor"),
        P("dp", "ctx", "tensor"),
        P(None, "tensor"),
        P(None, "tensor"),
        P("dp", None),
        P("dp", None, None),
        P("dp", None),
    )
    out_specs = (
        P("dp", "ctx", "tensor"),
        P("dp", ("ctx", "tensor"), None),
        P(("dp", "ctx"), "tensor"),
        P(("dp", "ctx"), "tensor"),
    )
    return jax.shard_map(
        per_device, mesh=mesh, in_specs=in_specs, out_specs=out_specs, check_vma=False
    )
```

```python
import functools
import math

import jax
import jax.numpy as jnp
from jax import lax
from jax.experimental import pallas as pl
from jax.experimental.pallas import tpu as pltpu
from jax.sharding import PartitionSpec as P

HEAD_SIZE = 128
BLK = 128

MESH = pl.DeviceIdType.MESH


def exchange_kernel(
    nt, nd, nc, x_ref, kw_ref, vw_ref, kv_ref, xc_ref, wide_ref,
    x_send, x_recv, w_send, w_recv, p_send, p_recv, f_send, f_recv, s_send, s_recv,
    k_send, k_recv, local_sem, g_ref, kw, vw, sums,
):
    t = lax.axis_index("tensor")
    d = lax.axis_index("dp")
    c = lax.axis_index("ctx")
    plane = nd * nc
    half = plane // 2
    p = d * nc + c
    h = (d // 2) * nc + c
    core = d % 2
    rows, width = x_ref.shape
    kv = kw_ref.shape[1]
    chunk = width // nt
    piece = chunk // plane
    slice_width = width // plane

    barrier = pltpu.get_barrier_semaphore()
    for r in range(1, nt):
        pl.semaphore_signal(
            barrier, inc=1, device_id={"tensor": (t + r) % nt}, device_id_type=MESH
        )
    for r in range(1, plane):
        q = (p + r) % plane
        pl.semaphore_signal(
            barrier, inc=1, device_id={"dp": q // nc, "ctx": q % nc}, device_id_type=MESH
        )
    pl.semaphore_wait(barrier, nt - 1 + plane - 1)

    def x_rows(b):
        return g_ref.at[pl.ds(pl.multiple_of(b * rows, rows), rows), :]

    def x_copy(way, s, source, b, target):
        return pltpu.make_async_remote_copy(
            src_ref=source, dst_ref=x_rows(b), send_sem=x_send.at[way, s - 1],
            recv_sem=x_recv.at[way, s - 1], device_id={"tensor": target}, device_id_type=MESH,
        )

    def sends(s):
        for way in (0, 1):
            step = 1 if way == 0 else -1
            b = t - step * (s - 1)
            target = t + step
            ok = (target >= 0) & (target < nt) & (b >= 0) & (b < nt)
            yield way, ok, b, target

    def start_x(s):
        for way, ok, b, target in sends(s):
            @pl.when(ok)
            def _():
                x_copy(way, s, x_ref if s == 1 else x_rows(b), b, target).start()

    def w_copy(which, r):
        other = (t + r) % nt
        source = (kw_ref, vw_ref)[which].at[
            pl.ds(pl.multiple_of(other * chunk + p * piece, piece), piece), :
        ]
        return pltpu.make_async_remote_copy(
            src_ref=source,
            dst_ref=wide_ref.at[
                t, pl.ds(pl.multiple_of(p * piece, piece), piece), pl.ds(which * kv, kv)
            ],
            send_sem=w_send.at[which, r - 1], recv_sem=w_recv.at[which, r - 1],
            device_id={"tensor": other}, device_id_type=MESH,
        )

    def plane_copy(b, r, source):
        q = (p + r) % plane
        return pltpu.make_async_remote_copy(
            src_ref=source.at[:, pl.ds(pl.multiple_of(q * slice_width, slice_width), slice_width)],
            dst_ref=xc_ref.at[p, b],
            send_sem=p_send.at[b, r - 1], recv_sem=p_recv.at[b, r - 1],
            device_id={"dp": q // nc, "ctx": q % nc}, device_id_type=MESH,
        )

    def keep_copy(b):
        return pltpu.make_async_copy(
            x_rows(b).at[:, pl.ds(pl.multiple_of(p * slice_width, slice_width), slice_width)],
            xc_ref.at[p, b], local_sem.at[3 + b],
        )

    def rows_of(i):
        return pl.ds(pl.multiple_of(i * nt * rows, nt * rows), nt * rows)

    def kv_copy(j):
        return pltpu.make_async_remote_copy(
            src_ref=kv_ref.at[rows_of(c), :], dst_ref=kv_ref.at[rows_of(c), :],
            send_sem=k_send.at[j - 1], recv_sem=k_recv.at[j - 1],
            device_id={"ctx": (c + j) % nc}, device_id_type=MESH,
        )

    def to_plane(b, source):
        for r in range(1, plane):
            plane_copy(b, r, source).start()

    def wide_at(r, q):
        return wide_ref.at[(t + nt - r) % nt, pl.ds(pl.multiple_of(q * piece, piece), piece), :]

    def fan_copy(r, j):
        hh = (h + j) % half
        return pltpu.make_async_remote_copy(
            src_ref=wide_at(r, p), dst_ref=wide_at(r, p),
            send_sem=f_send.at[r - 1, j - 1], recv_sem=f_recv.at[r - 1, j - 1],
            device_id={"dp": (hh // nc) * 2 + core, "ctx": hh % nc}, device_id_type=MESH,
        )

    def sibling_copy(r, j):
        hh = (h + half - j) % half
        q = ((hh // nc) * 2 + core) * nc + hh % nc
        return pltpu.make_async_remote_copy(
            src_ref=wide_at(r, q), dst_ref=wide_at(r, q),
            send_sem=s_send.at[r - 1, j], recv_sem=s_recv.at[r - 1, j],
            device_id={"dp": d + 1 - 2 * core}, device_id_type=MESH,
        )

    for r in range(1, nt):
        for which in (0, 1):
            w_copy(which, r).start()
    start_x(1)
    to_plane(t, x_ref)
    loads = [
        pltpu.make_async_copy(x_ref, x_rows(t), local_sem.at[0]),
        pltpu.make_async_copy(kw_ref, kw, local_sem.at[1]),
        pltpu.make_async_copy(vw_ref, vw, local_sem.at[2]),
    ]
    for copy in loads:
        copy.start()
    for copy in loads:
        copy.wait()
    keep_copy(t).start()
    own_chunk = pl.ds(pl.multiple_of(t * chunk, chunk), chunk)
    own = [
        pltpu.make_async_copy(
            kw.at[own_chunk, :], wide_ref.at[t, :, pl.ds(0, kv)], local_sem.at[1]
        ),
        pltpu.make_async_copy(
            vw.at[own_chunk, :], wide_ref.at[t, :, pl.ds(kv, kv)], local_sem.at[2]
        ),
    ]
    for copy in own:
        copy.start()
    for s in range(1, nt):
        for which in (0, 1):
            w_copy(which, s).wait_recv()
        for j in range(1, half):
            fan_copy(s, j).start()
        sibling_copy(s, 0).start()
    for s in range(1, nt):
        for way in (0, 1):
            b = t - s if way == 0 else t + s

            @pl.when((b >= 0) & (b < nt))
            def _():
                x_copy(way, s, x_ref, b, (t + 1) % nt).wait_recv()

        if s < nt - 1:
            start_x(s + 1)
        for way in (0, 1):
            b = t - s if way == 0 else t + s

            @pl.when((b >= 0) & (b < nt))
            def _():
                to_plane(b, x_rows(b))
                keep_copy(b).start()

        if s == nt - 2:
            for r in range(1, nt):
                for j in range(1, half):
                    fan_copy(r, j).wait_recv()
                    sibling_copy(r, j).start()
    sums[...] = jnp.zeros_like(sums)
    depth = min(1024, width)

    @pl.loop(0, width // depth)
    def _(i):
        part = pl.ds(pl.multiple_of(i * depth, depth), depth)
        left = g_ref[:, part]
        sums[:, :kv] += jnp.dot(left, kw[part, :], preferred_element_type=jnp.float32)
        sums[:, kv:] += jnp.dot(left, vw[part, :], preferred_element_type=jnp.float32)

    kv_ref[rows_of(c), :] = sums[...].astype(jnp.bfloat16)
    for j in range(1, nc):
        kv_copy(j).start()
    for j in range(1, nc):
        kv_copy(j).wait()
    for s in range(1, nt):
        for way, ok, b, target in sends(s):
            @pl.when(ok)
            def _():
                x_copy(way, s, x_ref, b, target).wait_send()
        for which in (0, 1):
            w_copy(which, s).wait_send()
        for j in range(1, half):
            fan_copy(s, j).wait_send()
        for j in range(half):
            sibling_copy(s, j).wait()
    for b in range(nt):
        for r in range(1, plane):
            plane_copy(b, r, x_ref).wait()
        keep_copy(b).wait()
    for copy in own:
        copy.wait()


def exchange_inputs(x, key_weight, value_weight):
    nt, nd, nc = lax.axis_size("tensor"), lax.axis_size("dp"), lax.axis_size("ctx")
    plane = nd * nc
    rows, width = x.shape
    kv = key_weight.shape[1]
    dma = pltpu.SemaphoreType.DMA
    return pl.pallas_call(
        functools.partial(exchange_kernel, nt, nd, nc),
        out_shape=(
            jax.ShapeDtypeStruct((nc * nt * rows, 2 * kv), x.dtype),
            jax.ShapeDtypeStruct((plane, nt, rows, width // plane), x.dtype),
            jax.ShapeDtypeStruct((nt, width // nt, 2 * kv), x.dtype),
        ),
        in_specs=[pl.BlockSpec(memory_space=pltpu.HBM)] * 3,
        out_specs=[
            pl.BlockSpec(memory_space=pltpu.VMEM),
            pl.BlockSpec(memory_space=pltpu.HBM),
            pl.BlockSpec(memory_space=pltpu.HBM),
        ],
        scratch_shapes=[
            dma((2, nt - 1)), dma((2, nt - 1)), dma((2, nt - 1)), dma((2, nt - 1)),
            dma((nt, plane - 1)), dma((nt, plane - 1)),
            dma((nt - 1, plane // 2 - 1)), dma((nt - 1, plane // 2 - 1)),
            dma((nt - 1, plane // 2)), dma((nt - 1, plane // 2)),
            dma((nc - 1,)), dma((nc - 1,)), dma((3 + nt,)),
            pltpu.VMEM((nt * rows, width), x.dtype),
            pltpu.VMEM((width, kv), x.dtype),
            pltpu.VMEM((width, kv), x.dtype),
            pltpu.VMEM((nt * rows, 2 * kv), jnp.float32),
        ],
        compiler_params=pltpu.CompilerParams(
            collective_id=0, has_side_effects=True, vmem_limit_bytes=48 << 20
        ),
    )(x, key_weight, value_weight)


def finish_kernel(
    nt, nd, nc, sum_ref, wide_ref, xc_ref, dx_ref, dw_ref,
    part, kz, kp, wide, xc, dx_send,
    c_send, c_recv, z_send, z_recv, p_send, p_recv, d_send, d_recv, local_sem,
):
    t = lax.axis_index("tensor")
    d = lax.axis_index("dp")
    c = lax.axis_index("ctx")
    plane = nd * nc
    p = d * nc + c
    group_rows = kz.shape[1]
    rows, chunk = dx_send.shape[1:]

    load_wide = pltpu.make_async_copy(wide_ref, wide, local_sem.at[0])
    load_xc = pltpu.make_async_copy(xc_ref, xc, local_sem.at[1])
    load_wide.start()
    load_xc.start()
    barrier = pltpu.get_barrier_semaphore()
    for r in range(1, nt):
        pl.semaphore_signal(
            barrier, inc=1, device_id={"tensor": (t + r) % nt}, device_id_type=MESH
        )
    for r in range(1, plane):
        q = (p + r) % plane
        pl.semaphore_signal(
            barrier, inc=1, device_id={"dp": q // nc, "ctx": q % nc}, device_id_type=MESH
        )
    pl.semaphore_wait(barrier, nt - 1 + plane - 1)

    def block(i):
        return pl.ds(pl.multiple_of(i * group_rows, group_rows), group_rows)

    span = group_rows // 2

    def half_block(i, e):
        return pl.ds(pl.multiple_of(i * group_rows + e * span, span), span)

    def part_copy(j, e):
        other = (c + j) % nc
        return pltpu.make_async_remote_copy(
            src_ref=sum_ref.at[half_block(other, e), :],
            dst_ref=part.at[j - 1, pl.ds(e * span, span), :],
            send_sem=c_send.at[e, j - 1], recv_sem=c_recv.at[e, j - 1],
            device_id={"ctx": other}, device_id_type=MESH,
        )

    def z_copy(r, e):
        own = kz.at[t, pl.ds(e * span, span), :]
        return pltpu.make_async_remote_copy(
            src_ref=own, dst_ref=own, send_sem=z_send.at[e, r - 1],
            recv_sem=z_recv.at[e, r - 1], device_id={"tensor": (t + r) % nt}, device_id_type=MESH,
        )

    def p_copy(r, e):
        q = (p + r) % plane
        return pltpu.make_async_remote_copy(
            src_ref=kz.at[t, pl.ds(e * span, span), :], dst_ref=kp.at[half_block(p, e), :],
            send_sem=p_send.at[e, r - 1], recv_sem=p_recv.at[e, r - 1], device_id={"dp": q // nc, "ctx": q % nc},
            device_id_type=MESH,
        )

    def dx_part(r):
        other = (t + r) % nt
        return pltpu.make_async_remote_copy(
            src_ref=dx_send.at[other],
            dst_ref=dx_ref.at[:, pl.ds(pl.multiple_of(t * chunk, chunk), chunk)],
            send_sem=d_send.at[r - 1], recv_sem=d_recv.at[r - 1],
            device_id={"tensor": other}, device_id_type=MESH,
        )

    for e in range(2):
        for j in range(1, nc):
            part_copy(j, e).start()
    for e in range(2):
        for j in range(1, nc):
            part_copy(j, e).wait_recv()
        total = sum_ref[half_block(c, e), :]
        for j in range(1, nc):
            total = total + part[j - 1, pl.ds(e * span, span), :]
        total = total.astype(jnp.bfloat16)
        kz[t, pl.ds(e * span, span), :] = total
        kp[half_block(p, e), :] = total
        for r in range(1, nt):
            z_copy(r, e).start()
        for r in range(1, plane):
            p_copy(r, e).start()
    load_wide.wait()
    tile = 256
    targets = nt // 2
    for e in range(2):
        for r in range(1, nt):
            z_copy(r, e).wait_recv()

        @pl.loop(0, chunk // tile)
        def _(n):
            columns = pl.ds(pl.multiple_of(n * tile, tile), tile)
            out = None
            for b in range(nt):
                term = lax.dot_general(
                    kz[b, pl.ds(e * span, span), :], wide[b, columns, :],
                    (((1,), (1,)), ((), ())), preferred_element_type=jnp.float32,
                )
                out = term if out is None else out + term
            dx_send[pl.ds(e * targets, targets), :, columns] = out.astype(
                jnp.bfloat16
            ).reshape(targets, rows, tile)

        for r in range(1, nt):
            @pl.when(((t + r) % nt) // targets == e)
            def _():
                dx_part(r).start()

    keep = pltpu.make_async_copy(
        dx_send.at[t], dx_ref.at[:, pl.ds(pl.multiple_of(t * chunk, chunk), chunk)],
        local_sem.at[2],
    )
    keep.start()
    load_xc.wait()
    for e in range(2):
        for r in range(1, plane):
            p_copy(r, e).wait_recv()

    @pl.loop(0, dw_ref.shape[0] // tile)
    def _(m):
        columns = pl.ds(pl.multiple_of(m * tile, tile), tile)
        out = lax.dot_general(
            xc[:, columns], kp[...], (((0,), (0,)), ((), ())),
            preferred_element_type=jnp.float32,
        )
        dw_ref[columns, :] = out.astype(jnp.bfloat16)

    for e in range(2):
        for j in range(1, nc):
            part_copy(j, e).wait_send()
        for r in range(1, nt):
            z_copy(r, e).wait_send()
        for r in range(1, plane):
            p_copy(r, e).wait_send()
    for r in range(1, nt):
        dx_part(r).wait()
    keep.wait()


def finish_grads(keyval_sum, wide_weight, plane_input):
    nt, nd, nc = lax.axis_size("tensor"), lax.axis_size("dp"), lax.axis_size("ctx")
    plane = nd * nc
    seq_rows, kv2 = keyval_sum.shape
    group_rows = seq_rows // nc
    chunk = wide_weight.shape[1]
    slice_width = plane_input.shape[1]
    low = plane_input.dtype
    dma = pltpu.SemaphoreType.DMA
    hbm = pl.BlockSpec(memory_space=pltpu.HBM)
    vmem = pl.BlockSpec(memory_space=pltpu.VMEM)
    return pl.pallas_call(
        functools.partial(finish_kernel, nt, nd, nc),
        out_shape=(
            jax.ShapeDtypeStruct((group_rows // nt, chunk * nt), low),
            jax.ShapeDtypeStruct((slice_width, kv2), low),
        ),
        in_specs=[vmem, hbm, hbm],
        out_specs=[hbm, vmem],
        scratch_shapes=[
            pltpu.VMEM((nc - 1, group_rows, kv2), jnp.float32),
            pltpu.VMEM((nt, group_rows, kv2), low),
            pltpu.VMEM((plane * group_rows, kv2), low),
            pltpu.VMEM(wide_weight.shape, low),
            pltpu.VMEM(plane_input.shape, low),
            pltpu.VMEM((nt, group_rows // nt, chunk), low),
            dma((2, nc - 1)), dma((2, nc - 1)), dma((2, nt - 1)), dma((2, nt - 1)),
            dma((2, plane - 1)), dma((2, plane - 1)), dma((nt - 1,)), dma((nt - 1,)), dma((3,)),
        ],
        compiler_params=pltpu.CompilerParams(
            collective_id=1, has_side_effects=True, vmem_limit_bytes=56 << 20
        ),
    )(keyval_sum, wide_weight, plane_input)


def per_device(
    layer_input,
    queries,
    forward_output,
    attention_output_gradient,
    key_weight,
    value_projection_weight,
    segment,
    block_table,
    block_owner,
):
    softmax_scale = 1.0 / math.sqrt(HEAD_SIZE)
    local_rows = queries.shape[1]
    kv_local = key_weight.shape[1] // HEAD_SIZE
    q_local = queries.shape[2] // HEAD_SIZE
    queries_per_group = q_local // kv_local
    kv_width = kv_local * HEAD_SIZE
    kv_full, plane_input, wide_weight = exchange_inputs(
        layer_input[0], key_weight, value_projection_weight
    )
    plane_input = plane_input.reshape(-1, plane_input.shape[3])
    owner_row = block_owner[0]
    segments_row = segment[0]
    table_row = block_table[0]
    blocks_here = local_rows // BLK
    ctx_index = lax.axis_index("ctx")
    own_blocks = lax.dynamic_slice_in_dim(owner_row, ctx_index * blocks_here, blocks_here)
    offsets = jnp.arange(BLK, dtype=jnp.int32)
    query_pos = (own_blocks[:, None] * BLK + offsets[None, :]).reshape(-1)
    block_ids = jnp.arange(owner_row.shape[0], dtype=jnp.int32)
    segment_blocks = segments_row.reshape(-1, BLK)

    def segments_of(blocks):
        chosen = (blocks[:, None] == block_ids[None, :])[:, :, None]
        return jnp.sum(jnp.where(chosen, segment_blocks[None], 0), axis=1).reshape(-1)

    query_seg = segments_of(own_blocks)
    own_chosen = (own_blocks[:, None] == block_ids[None, :])[:, :, None]
    own_table = jnp.sum(jnp.where(own_chosen, table_row[None], 0), axis=1)
    query_heads = queries[0].reshape(local_rows, kv_local, queries_per_group, HEAD_SIZE)
    grad_heads = attention_output_gradient[0].reshape(
        local_rows, kv_local, queries_per_group, HEAD_SIZE
    )
    saved_heads = forward_output[0].reshape(local_rows, kv_local, queries_per_group, HEAD_SIZE)
    correction = jnp.sum(grad_heads.astype(jnp.float32) * saved_heads.astype(jnp.float32), axis=-1)
    correction = correction.transpose(1, 2, 0)

    def allowed_for(leading_row, row_count):
        key_blocks = lax.dynamic_slice_in_dim(owner_row, leading_row // BLK, row_count // BLK)
        key_pos = (key_blocks[:, None] * BLK + offsets[None, :]).reshape(-1)
        key_seg = segments_of(key_blocks)
        key_chosen = (key_blocks[:, None] == block_ids[None, :])[None]
        table_part = jnp.sum(jnp.where(key_chosen, own_table[:, None, :], 0), axis=2) == 1
        table_full = jnp.broadcast_to(
            table_part[:, None, :, None], (blocks_here, BLK, row_count // BLK, BLK)
        )
        table_full = table_full.reshape(local_rows, row_count)
        same_tree = (key_seg[None, :] == 0) | (key_seg[None, :] == query_seg[:, None])
        return table_full & (key_pos[None, :] <= query_pos[:, None]) & same_tree

    def block_scores(block_rows, leading_row):
        row_count = block_rows.shape[0]
        block_keys = block_rows[:, :kv_width].reshape(row_count, kv_local, HEAD_SIZE)
        block_values = block_rows[:, kv_width:].reshape(row_count, kv_local, HEAD_SIZE)
        raw_scores = (
            jnp.einsum(
                "qhgd,khd->hgqk", query_heads, block_keys, preferred_element_type=jnp.float32
            )
            * softmax_scale
        )
        allowed = allowed_for(leading_row, row_count)
        return (jnp.where(allowed[None, None], raw_scores, -jnp.inf), block_keys, block_values)

    def stats_block(carried, block_rows, leading_row):
        running_max, running_sum = carried
        scores = block_scores(block_rows, leading_row)[0]
        new_max = jnp.maximum(running_max, jnp.max(scores, axis=-1))
        running_sum = running_sum * jnp.exp(running_max - new_max) + jnp.sum(
            jnp.exp(scores - new_max[..., None]), axis=-1
        )
        return (new_max, running_sum)

    def grads_block(carried, block_rows, leading_row, log_norm):
        query_sum, keyval_sum = carried
        row_count = block_rows.shape[0]
        scores, block_keys, block_values = block_scores(block_rows, leading_row)
        probabilities = jnp.exp(scores - log_norm[..., None])
        probs_low = probabilities.astype(jnp.bfloat16)
        value_gradient_rows = jnp.einsum(
            "hgqk,qhgd->khd", probs_low, grad_heads, preferred_element_type=jnp.float32
        )
        prob_grads = jnp.einsum(
            "qhgd,khd->hgqk", grad_heads, block_values, preferred_element_type=jnp.float32
        )
        score_low = (probabilities * (prob_grads - correction[..., None])).astype(jnp.bfloat16)
        query_sum = query_sum + jnp.einsum(
            "hgqk,khd->qhgd", score_low, block_keys, preferred_element_type=jnp.float32
        )
        key_gradient_rows = (
            jnp.einsum("hgqk,qhgd->khd", score_low, query_heads, preferred_element_type=jnp.float32)
            * softmax_scale
        )
        update = jnp.concatenate(
            [
                key_gradient_rows.reshape(row_count, kv_width),
                value_gradient_rows.reshape(row_count, kv_width),
            ],
            axis=1,
        )
        keyval_sum = lax.dynamic_update_slice_in_dim(keyval_sum, update, leading_row, 0)
        return (query_sum, keyval_sum)

    def over_blocks(block_step, carried, shard_part):
        row_count = shard_part.shape[0]
        block_size = math.gcd(row_count, max(512, local_rows))
        block_count = row_count // block_size
        pieces = shard_part.reshape(block_count, block_size, shard_part.shape[1])
        starts = block_size * jnp.arange(block_count, dtype=jnp.int32)

        def one_block(state_in, scan_item):
            block_rows, block_start = scan_item
            result = block_step(state_in, block_rows, block_start)
            return (result, None)

        carried, _ = lax.scan(one_block, carried, (pieces, starts))
        return carried

    stats_init = (
        jnp.full((kv_local, queries_per_group, local_rows), -1e30, jnp.float32),
        jnp.zeros((kv_local, queries_per_group, local_rows), jnp.float32),
    )
    seq_rows = local_rows * lax.axis_size("ctx")
    grads_init = (
        jnp.zeros((local_rows, kv_local, queries_per_group, HEAD_SIZE), jnp.float32),
        jnp.zeros((seq_rows, 2 * kv_width), jnp.float32),
    )
    running_max, running_sum = over_blocks(
        stats_block, stats_init, kv_full
    )
    log_norm = running_max + jnp.log(running_sum)

    def grads_fold(carried, shard_part):
        return over_blocks(
            lambda state, rows_in, start_in: grads_block(state, rows_in, start_in, log_norm),
            carried,
            shard_part,
        )

    query_sum, keyval_sum = grads_fold(
        grads_init, kv_full
    )
    query_grad = (
        (query_sum * softmax_scale).astype(jnp.bfloat16).reshape(1, local_rows, q_local * HEAD_SIZE)
    )
    input_grad, weight_grads = finish_grads(keyval_sum, wide_weight, plane_input)
    key_weight_grad = weight_grads[:, :kv_width]
    value_weight_grad = weight_grads[:, kv_width:]
    input_grad = input_grad[None]
    return (query_grad, input_grad, key_weight_grad, value_weight_grad)


def solution(mesh):
    in_specs = (
        P("dp", ("ctx", "tensor"), None),
        P("dp", "ctx", "tensor"),
        P("dp", "ctx", "tensor"),
        P("dp", "ctx", "tensor"),
        P(None, "tensor"),
        P(None, "tensor"),
        P("dp", None),
        P("dp", None, None),
        P("dp", None),
    )
    out_specs = (
        P("dp", "ctx", "tensor"),
        P("dp", ("ctx", "tensor"), None),
        P(("dp", "ctx"), "tensor"),
        P(("dp", "ctx"), "tensor"),
    )
    return jax.shard_map(
        per_device, mesh=mesh, in_specs=in_specs, out_specs=out_specs, check_vma=False
    )
```
